32 devices in a mesh: wide: 8 (over y, x, core), narrow: 4 (over z).
Axes of the slice: x: 2, y: 2, z: 4, core: 2. Of those that a mesh axis runs over, the one named last changes fastest.
Arguments:
- amps: float32 [1, 16, 640, 640], P(None, 'wide', 'narrow'), may hold values from -6 to 6
- cycle: float32 [16, 640, 5120], P(None, 'wide', 'narrow'), may hold values from -0.25 to 0.25
- irrep_i: int32 [1], replicated, may hold values from 0 to 7
- irrep_k: int32 [16], replicated, may hold values from 0 to 7, as said below
- irrep_j: int32 [8], replicated, may hold values from 0 to 7, as said below
- irrep_v: int32 [640], replicated, may hold values from 0 to 7, as said below
Outputs:
- cycle_term: float32 [1, 8, 640, 640], P(None, 'wide', 'narrow')
The draws below stay inside these ranges and needn't reach their ends.
Inputs may be any that keep to these rules, and one draw needn't show every extreme that they name: `irrep_k`: nondecreasing along the orbitals, the first 0 and the last 7. `irrep_j`: nondecreasing along the orbitals, the first 0 and the last 7. `irrep_v`: nondecreasing along the orbitals, the first 0 and the last 7.
All inputs are finite; a program needn't handle non-finite values.
Results may differ from the reference program's by a relative error of at most 0.000071.
Values sent between devices are 32-bit elements; how exact they have to be, the bound alone decides.
A program may use at most 64 MiB of HBM per device.

```python
import jax
import jax.numpy as jnp
from jax import lax

V = 640
OI = 1
OK = 16
OJ = 8


def sorted_labels(key, count):
    cuts = jnp.sort(jax.random.randint(key, (7,), 1, count))
    places = jnp.arange(count)
    return jnp.sum((places[:, None] >= cuts[None, :]).astype(jnp.int32), axis=1).astype(jnp.int32)


def draw_irrep_k(key, part):
    return sorted_labels(jax.random.fold_in(key, 11), OK)


def draw_irrep_j(key, part):
    return sorted_labels(jax.random.fold_in(key, 23), OJ)


def draw_irrep_v(key, part):
    return sorted_labels(jax.random.fold_in(key, 37), V)


def with_spikes(result, key, source, target, blocks, factor):
    def block_of(dim):
        return (jnp.arange(result.shape[dim]) // (result.shape[dim] // blocks)).reshape((-1,) + (1,) * (result.ndim - 1 - dim))

    near = jax.random.permutation(key, blocks)[block_of(target)]
    second = (block_of(target) + blocks // 2) % blocks
    return jnp.where((block_of(source) == near) | (block_of(source) == second), factor * result, result)


def block_scale(stream_key, shape, split, smallest, largest):
    loudness, own = 1.0, jax.random.fold_in(stream_key, 6)
    for axis_at, shards_of in split:
        draws = jnp.exp(jax.random.uniform(jax.random.fold_in(own, axis_at), (shards_of,), jnp.float32, smallest / len(split), largest / len(split)))
        loudness = loudness * jnp.repeat(draws, shape[axis_at] // shards_of).reshape([-1 if axis == axis_at else 1 for axis in range(len(shape))])
    return loudness


def centred(own_key, extent, deviation, most, pieces=(), dtype=jnp.bfloat16):
    gain = block_scale(own_key, extent, pieces, -0.22, 0.18) if pieces else 1.0
    drawn = jax.random.normal(own_key, extent, jnp.float32) * deviation * gain
    return jnp.minimum(jnp.maximum(drawn, -most), most).astype(dtype)


def bell_draw_with(own_key, shape, spread, limit, cuts, heavy, kind=jnp.bfloat16):
    entries = spread * jax.random.normal(own_key, shape, jnp.float32)
    if cuts:
        entries = entries * block_scale(own_key, shape, cuts, -0.22, 0.18)
    return jnp.clip(with_spikes(entries, jax.random.fold_in(own_key, 3), *heavy), -limit, limit).astype(kind)


def setup_inputs(seed: int = 0) -> dict:
    streams_of = jax.random.split(jax.random.key(seed), 7)
    amps = centred(streams_of[0], (OI, OK, V, V), 1.0, 6.0, ((1, 8), (2, 4)), jnp.float32)
    cycle = bell_draw_with(streams_of[1], (OK, V, V * OJ), (OK * V // 8) ** -0.5, 0.25, ((1, 8), (2, 4)), (1, 2, 8, 2.0), jnp.float32)
    irrep_i = jax.random.randint(streams_of[2], (OI,), 0, 8).astype(jnp.int32)
    irrep_k = draw_irrep_k(jax.random.fold_in(streams_of[6], 71), 0)
    irrep_j = draw_irrep_j(jax.random.fold_in(streams_of[6], 71), 0)
    irrep_v = draw_irrep_v(jax.random.fold_in(streams_of[6], 71), 0)
    return dict(amps=amps, cycle=cycle, irrep_i=irrep_i, irrep_k=irrep_k, irrep_j=irrep_j, irrep_v=irrep_v)


def reference(amps, cycle, irrep_i, irrep_k, irrep_j, irrep_v):
    cycle_full = cycle.reshape(OK, V, V, OJ)
    allowed_in = (irrep_i[:, None, None, None] ^ irrep_k[None, :, None, None] ^ irrep_v[None, None, :, None] ^ irrep_v[None, None, None, :]) == 0
    masked = jnp.where(allowed_in, amps, jnp.zeros_like(amps))
    product = jnp.einsum("ikac,kcbj->ijab", masked, cycle_full, precision=lax.Precision.HIGHEST)
    allowed_out = (irrep_i[:, None, None, None] ^ irrep_j[None, :, None, None] ^ irrep_v[None, None, :, None] ^ irrep_v[None, None, None, :]) == 0
    return jnp.where(allowed_out, product, jnp.zeros_like(product))
```

```python
import functools

import jax
import jax.numpy as jnp
from jax import lax
from jax.experimental import pallas as pl
from jax.experimental.pallas import tpu as pltpu
from jax.sharding import PartitionSpec as P

F32 = jnp.float32
BF16 = jnp.bfloat16
MESH = pl.DeviceIdType.MESH
UNIT = 16
ROWS = 256
VARIANTS = ((4, 4), (6, 4), (8, 4), (16, 8))


def pick(position, table):
    value = jnp.int32(table[0])
    for place in range(1, len(table)):
        value = jnp.where(position == place, jnp.int32(table[place]), value)
    return value


def near_first(count):
    return [sorted(range(count), key=lambda n: (abs(n - m), n if 2 * m < count else -n)) for m in range(count)]


def run_starts(labels, count):
    steps = count.bit_length()
    starts = []
    for g in range(1, 8):
        low, high = jnp.int32(0), jnp.int32(count)
        for _ in range(steps):
            middle = (low + high) // 2
            below = (labels[jnp.minimum(middle, count - 1)] < g) & (low < high)
            high = jnp.where(below | (low >= high), high, middle)
            low = jnp.where(below, middle + 1, low)
        starts.append(low)
    return starts


def labels_at(starts, places):
    total = jnp.zeros(places.shape, jnp.int32)
    for start in starts:
        total = total + jnp.where(places >= start, 1, 0)
    return total


def tiles_of(bl, al, parts):
    total = bl * al // 1024
    each = -(-total // parts)
    while parts > 1 and (total - each) % (parts - 1):
        each += 1
    return total, each, (total - each) // (parts - 1) if parts > 1 else 0


def cycle_kernel(slots, folds, wn, nn, amps_hbm, cycle, ir_i, ir_k, ir_j, ir_v, out,
                 amps, cyc, cth, ctl, amt, got, yb, xh, xl, acc, pk, ra, rb, snd, rc, out_t,
                 amps_sem, cyc_sem, s1, r1, zr, zl, zf, zw, ry, sa, rsa, sb, rsb, sc, rsc):
    w = lax.axis_index("wide")
    m = lax.axis_index("narrow")
    kl, al, vt = amps.shape
    kt, cl, bj = cyc.shape
    jt = wn
    bl = bj // jt
    groups = slots // kl
    lanes = 2 * kl * al
    chunks = cl // UNIT
    half = UNIT // 2
    parts = jt // folds
    total_tiles, each, step = tiles_of(bl, al, parts)
    pairs = wn // 2
    core = lax.rem(w, 2)
    chip = w // 2
    partner = w + 1 - 2 * core
    last = nn - 1
    edge = (m == 0) | (m == last)
    inner = (m > 0) & (m < last)

    load_amps = pltpu.make_async_copy(amps_hbm, amps, amps_sem)
    load_amps.start()
    load = pltpu.make_async_copy(cycle, cyc, cyc_sem)
    load.start()

    def slot_of_chip(p):
        return 2 * lax.rem(p, 2) + p // 2

    def owner_of(u):
        if parts == 1:
            return w
        if parts == 2:
            return 2 * slot_of_chip(lax.rem(w, folds)) + u
        return 2 * u + core

    barrier = pltpu.get_barrier_semaphore()
    for d in range(1, wn):
        pl.semaphore_signal(barrier, inc=1, device_id={"wide": lax.rem(w + d, wn)}, device_id_type=MESH)
    for d in range(1, nn):
        pl.semaphore_signal(barrier, inc=1, device_id={"narrow": lax.rem(m + d, nn)}, device_id_type=MESH)
    greeted = wn + nn - 2
    if parts > 1:
        greeted = greeted + parts * (nn - 1)
        for u in range(parts):
            for d in range(1, nn):
                pl.semaphore_signal(barrier, inc=1, device_id={"wide": owner_of(u), "narrow": lax.rem(m + d, nn)},
                                    device_id_type=MESH)

    label_i = ir_i[0]
    labels = [ir_k[k] for k in range(kt)]
    v_starts = run_starts(ir_v, vt)
    a_places = lax.broadcasted_iota(jnp.int32, (1, al), 1)

    def masks_of_own():
        return (labels_at(v_starts, lax.broadcasted_iota(jnp.int32, (vt, 1), 0))
                ^ labels_at(v_starts, a_places + m * al))

    load_amps.wait()
    ca = masks_of_own()
    for e in range(kl):
        turned = jnp.transpose(amps[e], (1, 0))
        kept = jnp.where(ca == (label_i ^ ir_k[w * kl + e]), turned, 0.0)
        for peer in range(wn):
            for n in range(chunks):
                for h in range(2):
                    here = peer * cl + n * UNIT + h * half
                    lane = (2 * e + h) * al
                    amt[peer, n * half:(n + 1) * half, lane:lane + al] = kept[here:here + half]

    pl.semaphore_wait(barrier, greeted)

    def rows_of(n):
        return pl.ds(pl.multiple_of(n * half, half), half)

    def first_copy(n, d):
        return pltpu.make_async_remote_copy(
            src_ref=amt.at[lax.rem(w + d, wn), rows_of(n)], dst_ref=got.at[w, rows_of(n)],
            send_sem=s1.at[n, d], recv_sem=r1.at[n, d], device_id={"wide": lax.rem(w + d, wn)}, device_id_type=MESH)

    for n in range(chunks):
        for d in range(1, wn):
            first_copy(n, d).start()
    got[w] = amt[w]

    if xh.shape[1] > al:
        xh[:, al:] = jnp.zeros((xh.shape[0], xh.shape[1] - al), BF16)
        xl[:, al:] = jnp.zeros((xl.shape[0], xl.shape[1] - al), BF16)
    load.wait()
    ks = 128 // UNIT

    @pl.loop(0, chunks)
    def _(n):
        here = pl.ds(pl.multiple_of(n * UNIT, UNIT), UNIT)
        for g in range(kt // ks):
            for col in range(bj // 128):
                block = cyc[g * ks:(g + 1) * ks, here, col * 128:(col + 1) * 128].reshape(128, 128)
                block = jnp.transpose(block, (1, 0))
                high = block.astype(BF16)
                cth[n, col * 128:(col + 1) * 128, g * 128:(g + 1) * 128] = high
                ctl[n, col * 128:(col + 1) * 128, g * 128:(g + 1) * 128] = (block - high.astype(F32)).astype(BF16)

    order = near_first(nn)
    flat = [order[z][t] for z in range(nn) for t in range(nn)]

    def block_at(t):
        return pick(m * nn + t, flat)

    def along(block, n, sem, target):
        return pltpu.make_async_remote_copy(
            src_ref=yb.at[block, rows_of(n)], dst_ref=yb.at[block, rows_of(n)], send_sem=sem,
            recv_sem=ry.at[block, n], device_id={"narrow": target}, device_id_type=MESH)

    def send_right(n):
        return along(m, n, zr.at[n], jnp.minimum(m + 1, last))

    def send_left(n):
        return along(m, n, zl.at[n], jnp.maximum(m - 1, 0))

    def send_far(n):
        return along(m, n, zf.at[n], jnp.where(m == 0, jnp.int32(2), jnp.int32(1)))

    def pass_on(f, n):
        block = jnp.where(m == 1, jnp.int32(2 + f), jnp.int32(1 - f))
        return along(block, n, zw.at[f, n], jnp.where(m == 1, jnp.int32(0), jnp.int32(last)))

    def forward(n):
        for f in range(2):
            copy = pass_on(f, n)
            copy.wait_recv()
            copy.start()

    def multiply(block, n):
        c_here = lax.broadcasted_iota(jnp.int32, (UNIT, 1), 0) + (w * cl + n * UNIT)
        pair = labels_at(v_starts, c_here) ^ labels_at(v_starts, a_places + block * al)
        for g in range(groups):
            for e in range(kl):
                lane = g * lanes + 2 * e * al
                value = jnp.concatenate(
                    [yb[block, rows_of(n), lane + h * al:lane + (h + 1) * al] for h in range(2)], axis=0)
                for src in range(g, wn, groups):
                    k = src * kl + e
                    mine = jnp.where(pair == (label_i ^ labels[k]), value, 0.0)
                    high = mine.astype(BF16)
                    xh[k * UNIT:(k + 1) * UNIT, :al] = high
                    xl[k * UNIT:(k + 1) * UNIT, :al] = (mine - high.astype(F32)).astype(BF16)
        for at in range(0, bj, ROWS):
            one = jnp.dot(cth[n, at:at + ROWS, :], xh[...], preferred_element_type=F32)
            two = jnp.dot(cth[n, at:at + ROWS, :], xl[...], preferred_element_type=F32)
            three = jnp.dot(ctl[n, at:at + ROWS, :], xh[...], preferred_element_type=F32)
            summed = one + (two + three)
            for x in range(acc.shape[0]):
                before = jnp.where(n > 0, acc[x, at:at + ROWS, :], 0.0)
                acc[x, at:at + ROWS, :] = before + summed[:, x * 128:(x + 1) * 128]

    def members(x):
        if folds == jt:
            return [2 * (x % pairs) + x // pairs]
        if parts == 2:
            x = 2 * (x % 2) + x // 2
        return list(range(x, jt, folds))

    def a_part(ref, t, c):
        if parts == 1:
            return ref.at[t, pl.ds(pairs * c, pairs)]
        if parts == 2:
            return ref.at[t, :, pl.ds(step * c, each)]
        return ref.at[t, pl.ds(c, 1)]

    def b_part(t, p):
        if parts == 1:
            return pk.at[t, pairs * core + p]
        if parts == 2:
            return pk.at[t, p, pl.ds(step * core, each)]
        return pk.at[t, core, pl.ds(step * p, each)]

    def stage_a(t):
        return pltpu.make_async_remote_copy(
            src_ref=a_part(pk, t, 1 - core), dst_ref=ra.at[t], send_sem=sa.at[t], recv_sem=rsa.at[t],
            device_id={"wide": partner}, device_id_type=MESH)

    def stage_b(t, d):
        there = lax.rem(chip + d, pairs)
        return pltpu.make_async_remote_copy(
            src_ref=b_part(t, there), dst_ref=rb.at[t, d - 1], send_sem=sb.at[t, d - 1], recv_sem=rsb.at[t, d - 1],
            device_id={"wide": 2 * there + core}, device_id_type=MESH)

    def target_of(q):
        if parts == 1:
            return w
        if parts == 2:
            return slot_of_chip(chip) + folds * q
        return core + folds * q

    def my_part():
        if parts == 1:
            return 0
        return core if parts == 2 else chip

    def stage_c(t, q, part):
        return pltpu.make_async_remote_copy(
            src_ref=snd.at[t], dst_ref=rc.at[m, part], send_sem=sc.at[t, q], recv_sem=rsc.at[m, part],
            device_id={"wide": target_of(q), "narrow": block_at(t)}, device_id_type=MESH)

    b_labels = labels_at(v_starts, lax.broadcasted_iota(jnp.int32, (bl, 1), 0) + m * bl) ^ label_i
    narrow_places = lax.broadcasted_iota(jnp.int32, (1, 128), 1)
    rest = al - 128
    turns = 128 // rest
    strip = bl // turns

    def pack(t, block):
        pair = [b_labels ^ labels_at(v_starts, narrow_places + (block * al + x * 128)) for x in range(2)]
        for x in range(folds):
            value = []
            for y in range(2):
                total = None
                for j in members(x):
                    here = acc[y, pl.ds(j, bl, stride=jt), :]
                    if parts > 1:
                        here = jnp.where(pair[y] == ir_j[j], here, 0.0 if total is None else total)
                    total = here
                value.append(total)
            whole = bl // 8
            pk[t, x, :whole] = value[0].reshape(whole, 8, 128)
            thin = jnp.concatenate([value[1][q * strip:(q + 1) * strip, :rest] for q in range(turns)], axis=1)
            pk[t, x, whole:] = thin.reshape(strip // 8, 8, 128)
        stage_a(t).start()

    def finish_a(t):
        stage_a(t).wait()
        mine = a_part(pk, t, core)
        mine[...] = mine[...] + ra[t]
        for d in range(1, pairs):
            stage_b(t, d).start()

    def finish_b(t):
        for d in range(1, pairs):
            stage_b(t, d).wait()
        total = b_part(t, chip)[...]
        for d in range(1, pairs):
            total = total + rb[t, d - 1]
        snd[t] = total
        for q in range(parts):
            here = (t == 0) & (target_of(q) == w)

            @pl.when(here)
            def _():
                rc[m, my_part()] = total

            @pl.when(jnp.logical_not(here))
            def _():
                stage_c(t, q, my_part()).start()

    lag = 2

    @pl.loop(0, chunks)
    def _(n):
        for d in range(1, wn):
            first_copy(n, d).wait()
        for g in range(groups):
            total = got[g, rows_of(n), :]
            for src in range(g + groups, wn, groups):
                total = total + got[src, rows_of(n), :]
            yb[m, rows_of(n), g * lanes:(g + 1) * lanes] = total

        @pl.when(m < last)
        def _():
            send_right(n).start()

        @pl.when(m > 0)
        def _():
            send_left(n).start()

        @pl.when(edge)
        def _():
            send_far(n).start()

        multiply(m, n)

        @pl.when(inner & (n >= lag))
        def _():
            forward(n - lag)

    pack(0, m)

    @pl.loop(1, nn)
    def _(t):
        block = block_at(t)

        @pl.loop(0, chunks)
        def _(n):
            @pl.when(inner & (t == 1) & (lax.rem(n, 2) == 0) & (n < 2 * lag))
            def _():
                forward(chunks - lag + n // 2)

            @pl.when(edge | (t == 1))
            def _():
                along(block, n, zr.at[n], m).wait_recv()

            multiply(block, n)

            @pl.when(n == 1)
            def _():
                finish_a(t - 1)

            @pl.when((n == 3) & (t >= 2))
            def _():
                finish_b(t - 2)

        pack(t, block)

    finish_a(last)
    finish_b(last - 1)
    finish_b(last)

    for z in range(nn):
        for u in range(parts):
            @pl.when(jnp.logical_not((m == z) & (owner_of(u) == w)))
            def _():
                pltpu.make_async_remote_copy(
                    src_ref=snd.at[0], dst_ref=rc.at[z, u], send_sem=sc.at[0, 0], recv_sem=rsc.at[z, u],
                    device_id={"wide": partner}, device_id_type=MESH).wait_recv()
    whole = bl // 8
    for z in range(nn):
        done = 0
        thin = []
        for u in range(parts):
            end = step * u + each
            top = min(end, whole)
            if done < top:
                out_t[z * bl + done * 8:z * bl + top * 8, :128] = (
                    rc[z, u, done - step * u:top - step * u].reshape((top - done) * 8, 128))
            low = max(done, whole)
            if low < end:
                thin.append(rc[z, u, low - step * u:end - step * u].reshape((end - low) * 8, 128))
            done = end
        thin = jnp.concatenate(thin, axis=0) if len(thin) > 1 else thin[0]
        for q in range(turns):
            base = z * bl + q * strip
            out_t[base:base + strip, 128:] = thin[:, q * rest:(q + 1) * rest]
    kept = jnp.where(masks_of_own() == (label_i ^ ir_j[w]), out_t[...], 0.0)
    out[...] = jnp.transpose(kept, (1, 0))

    for n in range(chunks):
        @pl.when(m < last)
        def _():
            send_right(n).wait_send()

        @pl.when(m > 0)
        def _():
            send_left(n).wait_send()

        @pl.when(edge)
        def _():
            send_far(n).wait_send()

        @pl.when(inner)
        def _():
            for f in range(2):
                pass_on(f, n).wait_send()
    for t in range(nn):
        for q in range(parts):
            @pl.when((t > 0) | (target_of(q) != w))
            def _():
                stage_c(t, q, my_part()).wait_send()


def packed_path(slots, folds, ident, amps, cycle, irrep_i, irrep_k, irrep_j, irrep_v):
    wn = lax.axis_size("wide")
    nn = lax.axis_size("narrow")
    _, kl, al, vt = amps.shape
    kt, cl, bj = cycle.shape
    bl = bj // wn
    groups = slots // kl
    lanes = 2 * kl * al
    chunks = cl // UNIT
    parts = wn // folds
    pairs = wn // 2
    total_tiles, each, _ = tiles_of(bl, al, parts)
    tile = (8, 128)
    first = {1: (pairs, total_tiles), 2: (folds, each), 4: (1, total_tiles)}[parts]
    wide_lanes = -(-al // 256) * 256
    vmem = pl.BlockSpec(memory_space=pltpu.VMEM)
    smem = pl.BlockSpec(memory_space=pltpu.SMEM)
    anywhere = pl.BlockSpec(memory_space=pl.ANY)
    dma = pltpu.SemaphoreType.DMA
    result = pl.pallas_call(
        functools.partial(cycle_kernel, slots, folds, wn, nn),
        out_shape=jax.ShapeDtypeStruct((al, vt), F32),
        in_specs=[anywhere, anywhere, smem, smem, smem, smem],
        out_specs=vmem,
        scratch_shapes=[
            pltpu.VMEM((kl, al, vt), F32),
            pltpu.VMEM((kt, cl, bj), F32),
            pltpu.VMEM((chunks, bj, kt * UNIT), BF16),
            pltpu.VMEM((chunks, bj, kt * UNIT), BF16),
            pltpu.VMEM((wn, cl // 2, lanes), F32),
            pltpu.VMEM((wn, cl // 2, lanes), F32),
            pltpu.VMEM((nn, cl // 2, groups * lanes), F32),
            pltpu.VMEM((kt * UNIT, wide_lanes), BF16),
            pltpu.VMEM((kt * UNIT, wide_lanes), BF16),
            pltpu.VMEM((wide_lanes // 128, bj, 128), F32),
            pltpu.VMEM((nn, folds, total_tiles) + tile, F32),
            pltpu.VMEM((nn,) + first + tile, F32),
            pltpu.VMEM((nn, pairs - 1, each) + tile, F32),
            pltpu.VMEM((nn, each) + tile, F32),
            pltpu.VMEM((nn, parts, each) + tile, F32),
            pltpu.VMEM((vt, al), F32),
            dma, dma, dma((chunks, wn)), dma((chunks, wn)), dma((chunks,)), dma((chunks,)), dma((chunks,)),
            dma((2, chunks)), dma((nn, chunks)), dma((nn,)), dma((nn,)), dma((nn, pairs - 1)), dma((nn, pairs - 1)),
            dma((nn, parts)), dma((nn, parts)),
        ],
        compiler_params=pltpu.CompilerParams(
            collective_id=ident, has_side_effects=True, vmem_limit_bytes=56 * 1024 * 1024),
    )(amps[0], cycle, irrep_i, irrep_k, irrep_j, irrep_v)
    return result.reshape(1, 1, al, vt)


def general_path(amps, cycle, irrep_i, irrep_k, irrep_j, irrep_v):
    wide_pos = lax.axis_index("wide")
    narrow_pos = lax.axis_index("narrow")
    wide_count = lax.axis_size("wide")
    narrow_count = lax.axis_size("narrow")
    i_total = amps.shape[0]
    k_local = amps.shape[1]
    a_local = amps.shape[2]
    v_total = amps.shape[3]
    k_total = cycle.shape[0]
    c_local = cycle.shape[1]
    b_local = v_total // narrow_count
    j_total = cycle.shape[2] // b_local
    j_local = j_total // wide_count
    cycle_four = cycle.reshape(k_total, c_local, b_local, j_total)
    k_labels = lax.dynamic_slice_in_dim(irrep_k, wide_pos * k_local, k_local)
    a_labels = lax.dynamic_slice_in_dim(irrep_v, narrow_pos * a_local, a_local)
    allowed_in = (
        irrep_i[:, None, None, None]
        ^ k_labels[None, :, None, None]
        ^ a_labels[None, None, :, None]
        ^ irrep_v[None, None, None, :]
        == 0
    )
    masked = jnp.where(allowed_in, amps, jnp.zeros_like(amps))
    moved = lax.all_to_all(masked, "wide", split_axis=3, concat_axis=1, tiled=True)
    piece = lax.all_gather(moved, "narrow", axis=2, tiled=True)
    part_sum = jnp.einsum("ikac,kcbj->iajb", piece, cycle_four, precision=lax.Precision.HIGHEST)
    terms = part_sum.reshape(piece.shape[0], piece.shape[2], j_total * b_local)
    summed = lax.psum_scatter(terms, "wide", scatter_dimension=2, tiled=True)
    summed_four = summed.reshape(i_total, v_total, j_local, b_local)
    j_labels = lax.dynamic_slice_in_dim(irrep_j, wide_pos * j_local, j_local)
    b_labels = lax.dynamic_slice_in_dim(irrep_v, narrow_pos * b_local, b_local)
    allowed_out = (
        irrep_i[:, None, None, None]
        ^ irrep_v[None, :, None, None]
        ^ j_labels[None, None, :, None]
        ^ b_labels[None, None, None, :]
        == 0
    )
    result = jnp.where(allowed_out, summed_four, jnp.zeros_like(summed_four)).reshape(
        i_total, v_total, j_local * b_local
    )
    returned = lax.all_to_all(result, "narrow", split_axis=1, concat_axis=2, tiled=True)
    spread = returned.reshape(i_total, a_local, narrow_count, j_local, b_local)
    return jnp.transpose(spread, (0, 3, 1, 2, 4)).reshape(i_total, j_local, a_local, v_total)


def level_kernel(labels_k, labels_j, out):
    def larger(labels, size):
        over = jnp.int32(0)
        for k in range(size, labels.shape[0]):
            over = over | jnp.where(labels[k] == labels[k - size], 1, 0)
        return over

    level = jnp.int32(0)
    missed = jnp.int32(1)
    for slots, folds in VARIANTS[:-1]:
        missed = missed & (larger(labels_k, slots) | larger(labels_j, folds))
        level = level + missed
    out[0] = level


def per_device(amps, cycle, irrep_i, irrep_k, irrep_j, irrep_v):
    wn = lax.axis_size("wide")
    nn = lax.axis_size("narrow")
    kt, cl, bj = cycle.shape
    al = amps.shape[2]
    bl = amps.shape[3] // nn
    fits = (amps.shape[0] == 1 and wn == 8 and nn == 4 and bj == bl * wn and bl == al and amps.shape[1] == 2
            and kt == 2 * wn and cl % UNIT == 0 and al == 160 and bj % ROWS == 0)
    if not fits:
        return general_path(amps, cycle, irrep_i, irrep_k, irrep_j, irrep_v)
    smem = pl.BlockSpec(memory_space=pltpu.SMEM)
    level = pl.pallas_call(
        level_kernel,
        out_shape=jax.ShapeDtypeStruct((1,), jnp.int32),
        in_specs=[smem, smem],
        out_specs=smem,
    )(irrep_k, irrep_j)[0]
    paths = [functools.partial(packed_path, *sizes, n) for n, sizes in enumerate(VARIANTS)]
    return lax.switch(level, paths, amps, cycle, irrep_i, irrep_k, irrep_j, irrep_v)


def solution(mesh):
    placed = (P(None, "wide", "narrow", None), P(None, "wide", "narrow"), P(), P(), P(), P())
    return jax.shard_map(
        per_device,
        mesh=mesh,
        in_specs=placed,
        out_specs=P(None, "wide", "narrow", None),
        check_vma=False,
    )
```

```python
import functools

import jax
import jax.numpy as jnp
from jax import lax
from jax.experimental import pallas as pl
from jax.experimental.pallas import tpu as pltpu
from jax.sharding import PartitionSpec as P

F32 = jnp.float32
BF16 = jnp.bfloat16
MESH = pl.DeviceIdType.MESH
UNIT = 16
ROWS = 256
VARIANTS = ((4, 4), (6, 4), (8, 4), (16, 8))
STEPS = ((0, 0), (0, 1), (0, 2), (0, 3), (0, 4), (1, 0), (1, 1), (3, 0), (1, 2), (3, 1), (1, 3), (1, 4),
         (2, 0), (2, 1), (2, 2), (2, 3), (2, 4), (3, 2), (3, 3), (3, 4))
FORWARD = (((0, 2), (0, 3), (0, 4), (1, 0), (1, 1)), ((3, 0), (1, 2), (3, 1), (1, 3), (1, 4)))
CROSS = ((0, 3), (0, 4), (1, 0), (1, 1), (3, 0))
NEAR = ((2, 1), (2, 2))
PAIRED = ((1, 1), (2, 0), (3, 2))
REDUCED = ((2, 1), (3, 2))


def pick(position, table):
    value = jnp.int32(table[0])
    for place in range(1, len(table)):
        if table[place] != table[0]:
            value = jnp.where(position == place, jnp.int32(table[place]), value)
    return value


def run_starts(labels, count):
    steps = count.bit_length()
    starts = []
    for g in range(1, 8):
        low, high = jnp.int32(0), jnp.int32(count)
        for _ in range(steps):
            middle = (low + high) // 2
            below = (labels[jnp.minimum(middle, count - 1)] < g) & (low < high)
            high = jnp.where(below | (low >= high), high, middle)
            low = jnp.where(below, middle + 1, low)
        starts.append(low)
    return starts


def labels_at(starts, places):
    total = jnp.zeros(places.shape, jnp.int32)
    for start in starts:
        total = total + jnp.where(places >= start, 1, 0)
    return total


def tiles_of(bl, al, parts):
    total = bl * al // 1024
    each = -(-total // parts)
    while parts > 1 and (total - each) % (parts - 1):
        each += 1
    return total, each, (total - each) // (parts - 1) if parts > 1 else 0


def cycle_kernel(slots, folds, wn, nn, amps_hbm, cycle, ir_i, ir_k, ir_j, ir_v, out,
                 amps, cyc, cth, ctl, amt, got, yb, xh, xl, acc, pk, ra, rb, snd, rc, out_t,
                 amps_sem, cyc_sem, s1, r1, zr, zf, zw, ry, sa, rsa, sb, rsb, sc, rsc):
    w = lax.axis_index("wide")
    m = lax.axis_index("narrow")
    kl, al, vt = amps.shape
    kt, cl, bj = cyc.shape
    jt = wn
    bl = bj // jt
    groups = slots // kl
    lanes = 2 * kl * al
    chunks = cl // UNIT
    half = UNIT // 2
    parts = jt // folds
    total_tiles, each, step = tiles_of(bl, al, parts)
    pairs = wn // 2
    core = lax.rem(w, 2)
    chip = w // 2
    partner = w + 1 - 2 * core
    inner = (m > 0) & (m < nn - 1)
    outer = jnp.logical_not(inner)
    near = m + 1 - 2 * lax.rem(m, 2)
    low = m < nn // 2
    cross = jnp.where(low, jnp.int32(2), jnp.int32(1))
    beyond = jnp.where(low, jnp.int32(3), jnp.int32(0))

    load_amps = pltpu.make_async_copy(amps_hbm, amps, amps_sem)
    load_amps.start()
    load = pltpu.make_async_copy(cycle, cyc, cyc_sem)

    def slot_of_chip(p):
        return 2 * lax.rem(p, 2) + p // 2

    def owner_of(u):
        if parts == 1:
            return w
        if parts == 2:
            return 2 * slot_of_chip(lax.rem(w, folds)) + u
        return 2 * u + core

    barrier = pltpu.get_barrier_semaphore()
    for d in range(1, wn):
        pl.semaphore_signal(barrier, inc=1, device_id={"wide": lax.rem(w + d, wn)}, device_id_type=MESH)
    for d in range(1, nn):
        pl.semaphore_signal(barrier, inc=1, device_id={"narrow": lax.rem(m + d, nn)}, device_id_type=MESH)
    greeted = wn + nn - 2
    if parts > 1:
        greeted = greeted + parts * (nn - 1)
        for u in range(parts):
            for d in range(1, nn):
                pl.semaphore_signal(barrier, inc=1, device_id={"wide": owner_of(u), "narrow": lax.rem(m + d, nn)},
                                    device_id_type=MESH)

    label_i = ir_i[0]
    labels = [ir_k[k] for k in range(kt)]
    v_starts = run_starts(ir_v, vt)
    a_places = lax.broadcasted_iota(jnp.int32, (1, al), 1)

    def masks_of_own():
        return (labels_at(v_starts, lax.broadcasted_iota(jnp.int32, (vt, 1), 0))
                ^ labels_at(v_starts, a_places + m * al))

    load_amps.wait()
    load.start()
    ca = masks_of_own()
    for e in range(kl):
        turned = jnp.transpose(amps[e], (1, 0))
        kept = jnp.where(ca == (label_i ^ ir_k[w * kl + e]), turned, 0.0)
        for peer in range(wn):
            for n in range(chunks):
                for h in range(2):
                    here = peer * cl + n * UNIT + h * half
                    lane = (2 * e + h) * al
                    amt[peer, n * half:(n + 1) * half, lane:lane + al] = kept[here:here + half]

    pl.semaphore_wait(barrier, greeted)

    def rows_of(n):
        return pl.ds(pl.multiple_of(n * half, half), half)

    def first_copy(n, d):
        return pltpu.make_async_remote_copy(
            src_ref=amt.at[lax.rem(w + d, wn), rows_of(n)], dst_ref=got.at[w, rows_of(n)],
            send_sem=s1.at[n, d], recv_sem=r1.at[n, d], device_id={"wide": lax.rem(w + d, wn)}, device_id_type=MESH)

    for n in range(chunks):
        for d in range(1, wn):
            first_copy(n, d).start()
    got[w] = amt[w]

    if xh.shape[1] > al:
        xh[:, al:] = jnp.zeros((xh.shape[0], xh.shape[1] - al), BF16)
        xl[:, al:] = jnp.zeros((xl.shape[0], xl.shape[1] - al), BF16)
    load.wait()
    ks = 128 // UNIT

    @pl.loop(0, chunks)
    def _(n):
        here = pl.ds(pl.multiple_of(n * UNIT, UNIT), UNIT)
        for g in range(kt // ks):
            for col in range(bj // 128):
                block = cyc[g * ks:(g + 1) * ks, here, col * 128:(col + 1) * 128].reshape(128, 128)
                block = jnp.transpose(block, (1, 0))
                high = block.astype(BF16)
                cth[n, col * 128:(col + 1) * 128, g * 128:(g + 1) * 128] = high
                ctl[n, col * 128:(col + 1) * 128, g * 128:(g + 1) * 128] = (block - high.astype(F32)).astype(BF16)

    def block_at(t):
        return jnp.where(t == 0, m, jnp.where(t == 1, cross, jnp.where(t == 2, beyond, near)))

    def along(block, n, sem, target):
        return pltpu.make_async_remote_copy(
            src_ref=yb.at[block, rows_of(n)], dst_ref=yb.at[block, rows_of(n)], send_sem=sem,
            recv_sem=ry.at[block, n], device_id={"narrow": target}, device_id_type=MESH)

    def send_cross(n):
        return along(m, n, zf.at[n], cross)

    def send_near(n):
        return along(m, n, zr.at[n], near)

    def pass_on(f, n):
        return along(beyond if f else cross, n, zw.at[f, n], near)

    def forward(f, n):
        copy = pass_on(f, n)
        copy.wait_recv()
        copy.start()

    def multiply(block, n, bank):
        c_here = lax.broadcasted_iota(jnp.int32, (UNIT, 1), 0) + (w * cl + n * UNIT)
        pair = labels_at(v_starts, c_here) ^ labels_at(v_starts, a_places + block * al)
        for g in range(groups):
            for e in range(kl):
                lane = g * lanes + 2 * e * al
                value = jnp.concatenate(
                    [yb[block, rows_of(n), lane + h * al:lane + (h + 1) * al] for h in range(2)], axis=0)
                for src in range(g, wn, groups):
                    k = src * kl + e
                    mine = jnp.where(pair == (label_i ^ labels[k]), value, 0.0)
                    high = mine.astype(BF16)
                    xh[k * UNIT:(k + 1) * UNIT, :al] = high
                    xl[k * UNIT:(k + 1) * UNIT, :al] = (mine - high.astype(F32)).astype(BF16)
        right = jnp.concatenate([xh[...], xl[...], xh[...]], axis=0)
        for at in range(0, bj, ROWS):
            high = cth[n, at:at + ROWS, :]
            left = jnp.concatenate([ctl[n, at:at + ROWS, :], high, high], axis=1)
            summed = jnp.dot(left, right, preferred_element_type=F32)
            for x in range(acc.shape[1]):
                before = jnp.where(n > 0, acc[bank, x, at:at + ROWS, :], 0.0)
                acc[bank, x, at:at + ROWS, :] = before + summed[:, x * 128:(x + 1) * 128]

    def members(x):
        if folds == jt:
            return [2 * (x % pairs) + x // pairs]
        if parts == 2:
            x = 2 * (x % 2) + x // 2
        return list(range(x, jt, folds))

    def a_part(ref, t, c):
        if parts == 1:
            return ref.at[t, pl.ds(pairs * c, pairs)]
        if parts == 2:
            return ref.at[t, :, pl.ds(step * c, each)]
        return ref.at[t, pl.ds(c, 1)]

    def b_part(t, p):
        if parts == 1:
            return pk.at[t, pairs * core + p]
        if parts == 2:
            return pk.at[t, p, pl.ds(step * core, each)]
        return pk.at[t, core, pl.ds(step * p, each)]

    def stage_a(t):
        return pltpu.make_async_remote_copy(
            src_ref=a_part(pk, t, 1 - core), dst_ref=ra.at[t], send_sem=sa.at[t], recv_sem=rsa.at[t],
            device_id={"wide": partner}, device_id_type=MESH)

    def stage_b(t, d):
        there = lax.rem(chip + d, pairs)
        return pltpu.make_async_remote_copy(
            src_ref=b_part(t, there), dst_ref=rb.at[t, d - 1], send_sem=sb.at[t, d - 1], recv_sem=rsb.at[t, d - 1],
            device_id={"wide": 2 * there + core}, device_id_type=MESH)

    def target_of(q):
        if parts == 1:
            return w
        if parts == 2:
            return slot_of_chip(chip) + folds * q
        return core + folds * q

    def my_part():
        if parts == 1:
            return 0
        return core if parts == 2 else chip

    def stage_c(t, q, part):
        return pltpu.make_async_remote_copy(
            src_ref=snd.at[t], dst_ref=rc.at[m, part], send_sem=sc.at[t, q], recv_sem=rsc.at[m, part],
            device_id={"wide": target_of(q), "narrow": block_at(t)}, device_id_type=MESH)

    b_labels = labels_at(v_starts, lax.broadcasted_iota(jnp.int32, (bl, 1), 0) + m * bl) ^ label_i
    narrow_places = lax.broadcasted_iota(jnp.int32, (1, 128), 1)
    rest = al - 128
    turns = 128 // rest
    strip = bl // turns

    def pack(t, block, bank):
        pair = [b_labels ^ labels_at(v_starts, narrow_places + (block * al + x * 128)) for x in range(2)]
        for x in range(folds):
            value = []
            for y in range(2):
                total = None
                for j in members(x):
                    here = acc[bank, y, pl.ds(j, bl, stride=jt), :]
                    if parts > 1:
                        here = jnp.where(pair[y] == ir_j[j], here, 0.0 if total is None else total)
                    total = here
                value.append(total)
            whole = bl // 8
            pk[t, x, :whole] = value[0].reshape(whole, 8, 128)
            thin = jnp.concatenate([value[1][q * strip:(q + 1) * strip, :rest] for q in range(turns)], axis=1)
            pk[t, x, whole:] = thin.reshape(strip // 8, 8, 128)
        stage_a(t).start()

    def finish_a(t):
        stage_a(t).wait()
        mine = a_part(pk, t, core)
        mine[...] = mine[...] + ra[t]
        for d in range(1, pairs):
            stage_b(t, d).start()

    def finish_b(t):
        for d in range(1, pairs):
            stage_b(t, d).wait()
        total = b_part(t, chip)[...]
        for d in range(1, pairs):
            total = total + rb[t, d - 1]
        snd[t] = total
        for q in range(parts):
            here = (t == 0) & (target_of(q) == w)

            @pl.when(here)
            def _():
                rc[m, my_part()] = total

            @pl.when(jnp.logical_not(here))
            def _():
                stage_c(t, q, my_part()).start()

    def take_own(n):
        for d in range(1, wn):
            first_copy(n, d).wait()
        for g in range(groups):
            total = got[g, rows_of(n), :]
            for src in range(g + groups, wn, groups):
                total = total + got[src, rows_of(n), :]
            yb[m, rows_of(n), g * lanes:(g + 1) * lanes] = total

        @pl.when(inner)
        def _():
            send_cross(n).start()

        @pl.when(outer | (n < 3))
        def _():
            send_near(n).start()

    def after(step, *places):
        chosen = step == STEPS.index(places[0])
        for place in places[1:]:
            chosen = chosen | (step == STEPS.index(place))
        return chosen

    @pl.loop(0, len(STEPS))
    def _(step):
        kind = pick(step, [k for k, _ in STEPS])
        n = pick(step, [c for _, c in STEPS])
        block = block_at(kind)
        bank = jnp.where(kind == 3, 1, 0)

        @pl.when(kind == 0)
        def _():
            take_own(n)

        @pl.when((kind == 3) | (outer & (kind > 0)))
        def _():
            along(block, n, zr.at[n], m).wait_recv()

        multiply(block, n, bank)

        for f, table in enumerate(FORWARD):
            @pl.when(inner & after(step, *table))
            def _():
                forward(f, pick(step, [table.index(p) if p in table else 0 for p in STEPS]))

        @pl.when(outer & after(step, *CROSS))
        def _():
            send_cross(pick(step, [CROSS.index(p) if p in CROSS else 0 for p in STEPS])).start()

        @pl.when(inner & after(step, *NEAR))
        def _():
            send_near(pick(step, [3 + NEAR.index(p) if p in NEAR else 3 for p in STEPS])).start()

        @pl.when(after(step, *PAIRED))
        def _():
            finish_a(pick(step, [PAIRED.index(p) if p in PAIRED else 0 for p in STEPS]))

        @pl.when(after(step, *REDUCED))
        def _():
            finish_b(pick(step, [REDUCED.index(p) if p in REDUCED else 0 for p in STEPS]))

        @pl.when(after(step, *[max((p for p in STEPS if p[0] == k), key=STEPS.index) for k in range(4)]))
        def _():
            pack(kind, block, bank)

    finish_a(nn - 1)
    finish_b(nn - 2)
    finish_b(nn - 1)

    for z in range(nn):
        for u in range(parts):
            @pl.when(jnp.logical_not((m == z) & (owner_of(u) == w)))
            def _():
                pltpu.make_async_remote_copy(
                    src_ref=snd.at[0], dst_ref=rc.at[z, u], send_sem=sc.at[0, 0], recv_sem=rsc.at[z, u],
                    device_id={"wide": partner}, device_id_type=MESH).wait_recv()
    whole = bl // 8
    for z in range(nn):
        done = 0
        thin = []
        for u in range(parts):
            end = step * u + each
            top = min(end, whole)
            if done < top:
                out_t[z * bl + done * 8:z * bl + top * 8, :128] = (
                    rc[z, u, done - step * u:top - step * u].reshape((top - done) * 8, 128))
            low = max(done, whole)
            if low < end:
                thin.append(rc[z, u, low - step * u:end - step * u].reshape((end - low) * 8, 128))
            done = end
        thin = jnp.concatenate(thin, axis=0) if len(thin) > 1 else thin[0]
        for q in range(turns):
            base = z * bl + q * strip
            out_t[base:base + strip, 128:] = thin[:, q * rest:(q + 1) * rest]
    kept = jnp.where(masks_of_own() == (label_i ^ ir_j[w]), out_t[...], 0.0)
    out[...] = jnp.transpose(kept, (1, 0))

    for n in range(chunks):
        send_cross(n).wait_send()
        send_near(n).wait_send()

        @pl.when(inner)
        def _():
            for f in range(2):
                pass_on(f, n).wait_send()
    for t in range(nn):
        for q in range(parts):
            @pl.when((t > 0) | (target_of(q) != w))
            def _():
                stage_c(t, q, my_part()).wait_send()


def packed_path(slots, folds, ident, amps, cycle, irrep_i, irrep_k, irrep_j, irrep_v):
    wn = lax.axis_size("wide")
    nn = lax.axis_size("narrow")
    _, kl, al, vt = amps.shape
    kt, cl, bj = cycle.shape
    bl = bj // wn
    groups = slots // kl
    lanes = 2 * kl * al
    chunks = cl // UNIT
    parts = wn // folds
    pairs = wn // 2
    total_tiles, each, _ = tiles_of(bl, al, parts)
    tile = (8, 128)
    first = {1: (pairs, total_tiles), 2: (folds, each), 4: (1, total_tiles)}[parts]
    wide_lanes = -(-al // 256) * 256
    vmem = pl.BlockSpec(memory_space=pltpu.VMEM)
    smem = pl.BlockSpec(memory_space=pltpu.SMEM)
    anywhere = pl.BlockSpec(memory_space=pl.ANY)
    dma = pltpu.SemaphoreType.DMA
    result = pl.pallas_call(
        functools.partial(cycle_kernel, slots, folds, wn, nn),
        out_shape=jax.ShapeDtypeStruct((al, vt), F32),
        in_specs=[anywhere, anywhere, smem, smem, smem, smem],
        out_specs=vmem,
        scratch_shapes=[
            pltpu.VMEM((kl, al, vt), F32),
            pltpu.VMEM((kt, cl, bj), F32),
            pltpu.VMEM((chunks, bj, kt * UNIT), BF16),
            pltpu.VMEM((chunks, bj, kt * UNIT), BF16),
            pltpu.VMEM((wn, cl // 2, lanes), F32),
            pltpu.VMEM((wn, cl // 2, lanes), F32),
            pltpu.VMEM((nn, cl // 2, groups * lanes), F32),
            pltpu.VMEM((kt * UNIT, wide_lanes), BF16),
            pltpu.VMEM((kt * UNIT, wide_lanes), BF16),
            pltpu.VMEM((2, wide_lanes // 128, bj, 128), F32),
            pltpu.VMEM((nn, folds, total_tiles) + tile, F32),
            pltpu.VMEM((nn,) + first + tile, F32),
            pltpu.VMEM((nn, pairs - 1, each) + tile, F32),
            pltpu.VMEM((nn, each) + tile, F32),
            pltpu.VMEM((nn, parts, each) + tile, F32),
            pltpu.VMEM((vt, al), F32),
            dma, dma, dma((chunks, wn)), dma((chunks, wn)), dma((chunks,)), dma((chunks,)),
            dma((2, chunks)), dma((nn, chunks)), dma((nn,)), dma((nn,)), dma((nn, pairs - 1)), dma((nn, pairs - 1)),
            dma((nn, parts)), dma((nn, parts)),
        ],
        compiler_params=pltpu.CompilerParams(
            collective_id=ident, has_side_effects=True, vmem_limit_bytes=56 * 1024 * 1024),
    )(amps[0], cycle, irrep_i, irrep_k, irrep_j, irrep_v)
    return result.reshape(1, 1, al, vt)


def general_path(amps, cycle, irrep_i, irrep_k, irrep_j, irrep_v):
    wide_pos = lax.axis_index("wide")
    narrow_pos = lax.axis_index("narrow")
    wide_count = lax.axis_size("wide")
    narrow_count = lax.axis_size("narrow")
    i_total = amps.shape[0]
    k_local = amps.shape[1]
    a_local = amps.shape[2]
    v_total = amps.shape[3]
    k_total = cycle.shape[0]
    c_local = cycle.shape[1]
    b_local = v_total // narrow_count
    j_total = cycle.shape[2] // b_local
    j_local = j_total // wide_count
    cycle_four = cycle.reshape(k_total, c_local, b_local, j_total)
    k_labels = lax.dynamic_slice_in_dim(irrep_k, wide_pos * k_local, k_local)
    a_labels = lax.dynamic_slice_in_dim(irrep_v, narrow_pos * a_local, a_local)
    allowed_in = (
        irrep_i[:, None, None, None]
        ^ k_labels[None, :, None, None]
        ^ a_labels[None, None, :, None]
        ^ irrep_v[None, None, None, :]
        == 0
    )
    masked = jnp.where(allowed_in, amps, jnp.zeros_like(amps))
    moved = lax.all_to_all(masked, "wide", split_axis=3, concat_axis=1, tiled=True)
    piece = lax.all_gather(moved, "narrow", axis=2, tiled=True)
    part_sum = jnp.einsum("ikac,kcbj->iajb", piece, cycle_four, precision=lax.Precision.HIGHEST)
    terms = part_sum.reshape(piece.shape[0], piece.shape[2], j_total * b_local)
    summed = lax.psum_scatter(terms, "wide", scatter_dimension=2, tiled=True)
    summed_four = summed.reshape(i_total, v_total, j_local, b_local)
    j_labels = lax.dynamic_slice_in_dim(irrep_j, wide_pos * j_local, j_local)
    b_labels = lax.dynamic_slice_in_dim(irrep_v, narrow_pos * b_local, b_local)
    allowed_out = (
        irrep_i[:, None, None, None]
        ^ irrep_v[None, :, None, None]
        ^ j_labels[None, None, :, None]
        ^ b_labels[None, None, None, :]
        == 0
    )
    result = jnp.where(allowed_out, summed_four, jnp.zeros_like(summed_four)).reshape(
        i_total, v_total, j_local * b_local
    )
    returned = lax.all_to_all(result, "narrow", split_axis=1, concat_axis=2, tiled=True)
    spread = returned.reshape(i_total, a_local, narrow_count, j_local, b_local)
    return jnp.transpose(spread, (0, 3, 1, 2, 4)).reshape(i_total, j_local, a_local, v_total)


def level_kernel(labels_k, labels_j, out):
    def larger(labels, size):
        over = jnp.int32(0)
        for k in range(size, labels.shape[0]):
            over = over | jnp.where(labels[k] == labels[k - size], 1, 0)
        return over

    level = jnp.int32(0)
    missed = jnp.int32(1)
    for slots, folds in VARIANTS[:-1]:
        missed = missed & (larger(labels_k, slots) | larger(labels_j, folds))
        level = level + missed
    out[0] = level


def per_device(amps, cycle, irrep_i, irrep_k, irrep_j, irrep_v):
    wn = lax.axis_size("wide")
    nn = lax.axis_size("narrow")
    kt, cl, bj = cycle.shape
    al = amps.shape[2]
    bl = amps.shape[3] // nn
    fits = (amps.shape[0] == 1 and wn == 8 and nn == 4 and bj == bl * wn and bl == al and amps.shape[1] == 2
            and kt == 2 * wn and cl == 5 * UNIT and al == 160 and bj % ROWS == 0)
    if not fits:
        return general_path(amps, cycle, irrep_i, irrep_k, irrep_j, irrep_v)
    smem = pl.BlockSpec(memory_space=pltpu.SMEM)
    level = pl.pallas_call(
        level_kernel,
        out_shape=jax.ShapeDtypeStruct((1,), jnp.int32),
        in_specs=[smem, smem],
        out_specs=smem,
    )(irrep_k, irrep_j)[0]
    paths = [functools.partial(packed_path, *sizes, n) for n, sizes in enumerate(VARIANTS)]
    return lax.switch(level, paths, amps, cycle, irrep_i, irrep_k, irrep_j, irrep_v)


def solution(mesh):
    placed = (P(None, "wide", "narrow", None), P(None, "wide", "narrow"), P(), P(), P(), P())
    return jax.shard_map(
        per_device,
        mesh=mesh,
        in_specs=placed,
        out_specs=P(None, "wide", "narrow", None),
        check_vma=False,
    )
```

```python
import functools

import jax
import jax.numpy as jnp
from jax import lax
from jax.experimental import pallas as pl
from jax.experimental.pallas import tpu as pltpu
from jax.sharding import PartitionSpec as P

F32 = jnp.float32
BF16 = jnp.bfloat16
MESH = pl.DeviceIdType.MESH
UNIT = 16
ROWS = 256
VARIANTS = ((4, 4), (5, 4), (6, 4), (7, 4), (8, 4), (16, 8))
STEPS = ((0, 0), (0, 1), (0, 2), (0, 3), (0, 4), (1, 0), (1, 1), (3, 0), (1, 2), (3, 1), (1, 3), (1, 4),
         (2, 0), (2, 1), (2, 2), (2, 3), (2, 4), (3, 2), (3, 3), (3, 4))
FORWARD = (((0, 2), (0, 3), (0, 4), (1, 0), (1, 1)), ((3, 0), (1, 2), (3, 1), (1, 3), (1, 4)))
CROSS = ((0, 3), (0, 4), (1, 0), (1, 1), (3, 0))
NEAR = ((2, 1), (2, 2))
PAIRED = ((1, 1), (2, 0), (3, 2))
REDUCED = ((2, 1), (3, 2))


def pick(position, table):
    value = jnp.int32(table[0])
    for place in range(1, len(table)):
        if table[place] != table[0]:
            value = jnp.where(position == place, jnp.int32(table[place]), value)
    return value


def run_starts(labels, count):
    steps = count.bit_length()
    starts = []
    for g in range(1, 8):
        low, high = jnp.int32(0), jnp.int32(count)
        for _ in range(steps):
            middle = (low + high) // 2
            below = (labels[jnp.minimum(middle, count - 1)] < g) & (low < high)
            high = jnp.where(below | (low >= high), high, middle)
            low = jnp.where(below, middle + 1, low)
        starts.append(low)
    return starts


def labels_at(starts, places):
    total = jnp.zeros(places.shape, jnp.int32)
    for start in starts:
        total = total + jnp.where(places >= start, 1, 0)
    return total


def tiles_of(bl, al, parts):
    total = bl * al // 1024
    each = -(-total // parts)
    while parts > 1 and (total - each) % (parts - 1):
        each += 1
    return total, each, (total - each) // (parts - 1) if parts > 1 else 0


def cycle_kernel(slots, folds, wn, nn, amps_hbm, cycle, ir_i, ir_k, ir_j, ir_v, out,
                 amps, cyc, cth, ctl, amt, got, yb, xh, xl, acc, pk, ra, rb, snd, rc, out_t,
                 amps_sem, cyc_sem, s1, r1, zr, zf, zw, ry, sa, rsa, sb, rsb, sc, rsc):
    w = lax.axis_index("wide")
    m = lax.axis_index("narrow")
    kl, al, vt = amps.shape
    kt, cl, bj = cyc.shape
    jt = wn
    bl = bj // jt
    chunks = cl // UNIT
    half = UNIT // 2
    parts = jt // folds
    total_tiles, each, step = tiles_of(bl, al, parts)
    pairs = wn // 2
    core = lax.rem(w, 2)
    chip = w // 2
    partner = w + 1 - 2 * core
    inner = (m > 0) & (m < nn - 1)
    outer = jnp.logical_not(inner)
    near = m + 1 - 2 * lax.rem(m, 2)
    low = m < nn // 2
    cross = jnp.where(low, jnp.int32(2), jnp.int32(1))
    beyond = jnp.where(low, jnp.int32(3), jnp.int32(0))

    load_amps = pltpu.make_async_copy(amps_hbm, amps, amps_sem)
    load_amps.start()
    load = pltpu.make_async_copy(cycle, cyc, cyc_sem)

    def slot_of_chip(p):
        return 2 * lax.rem(p, 2) + p // 2

    def owner_of(u):
        if parts == 1:
            return w
        if parts == 2:
            return 2 * slot_of_chip(lax.rem(w, folds)) + u
        return 2 * u + core

    barrier = pltpu.get_barrier_semaphore()
    for d in range(1, wn):
        pl.semaphore_signal(barrier, inc=1, device_id={"wide": lax.rem(w + d, wn)}, device_id_type=MESH)
    for d in range(1, nn):
        pl.semaphore_signal(barrier, inc=1, device_id={"narrow": lax.rem(m + d, nn)}, device_id_type=MESH)
    greeted = wn + nn - 2
    if parts > 1:
        greeted = greeted + parts * (nn - 1)
        for u in range(parts):
            for d in range(1, nn):
                pl.semaphore_signal(barrier, inc=1, device_id={"wide": owner_of(u), "narrow": lax.rem(m + d, nn)},
                                    device_id_type=MESH)

    label_i = ir_i[0]
    labels = [ir_k[k] for k in range(kt)]
    v_starts = run_starts(ir_v, vt)
    a_places = lax.broadcasted_iota(jnp.int32, (1, al), 1)

    def masks_of_own():
        return (labels_at(v_starts, lax.broadcasted_iota(jnp.int32, (vt, 1), 0))
                ^ labels_at(v_starts, a_places + m * al))

    load_amps.wait()
    load.start()
    ca = masks_of_own()
    for e in range(kl):
        turned = jnp.transpose(amps[e], (1, 0))
        kept = jnp.where(ca == (label_i ^ ir_k[w * kl + e]), turned, 0.0)
        for peer in range(wn):
            for n in range(chunks):
                for h in range(2):
                    here = peer * cl + n * UNIT + h * half
                    lane = (2 * e + h) * al
                    amt[peer, n * half:(n + 1) * half, lane:lane + al] = kept[here:here + half]

    pl.semaphore_wait(barrier, greeted)

    def rows_of(n):
        return pl.ds(pl.multiple_of(n * half, half), half)

    def first_copy(n, d):
        return pltpu.make_async_remote_copy(
            src_ref=amt.at[lax.rem(w + d, wn), rows_of(n)], dst_ref=got.at[w, rows_of(n)],
            send_sem=s1.at[n, d], recv_sem=r1.at[n, d], device_id={"wide": lax.rem(w + d, wn)}, device_id_type=MESH)

    for n in range(chunks):
        for d in range(1, wn):
            first_copy(n, d).start()
    got[w] = amt[w]

    if xh.shape[1] > al:
        xh[:, al:] = jnp.zeros((xh.shape[0], xh.shape[1] - al), BF16)
        xl[:, al:] = jnp.zeros((xl.shape[0], xl.shape[1] - al), BF16)
    load.wait()
    ks = 128 // UNIT

    @pl.loop(0, chunks)
    def _(n):
        here = pl.ds(pl.multiple_of(n * UNIT, UNIT), UNIT)
        for g in range(kt // ks):
            for col in range(bj // 128):
                block = cyc[g * ks:(g + 1) * ks, here, col * 128:(col + 1) * 128].reshape(128, 128)
                block = jnp.transpose(block, (1, 0))
                high = block.astype(BF16)
                cth[n, col * 128:(col + 1) * 128, g * 128:(g + 1) * 128] = high
                ctl[n, col * 128:(col + 1) * 128, g * 128:(g + 1) * 128] = (block - high.astype(F32)).astype(BF16)

    def block_at(t):
        return jnp.where(t == 0, m, jnp.where(t == 1, cross, jnp.where(t == 2, beyond, near)))

    def along(block, n, sem, target):
        return pltpu.make_async_remote_copy(
            src_ref=yb.at[block, rows_of(n)], dst_ref=yb.at[block, rows_of(n)], send_sem=sem,
            recv_sem=ry.at[block, n], device_id={"narrow": target}, device_id_type=MESH)

    def send_cross(n):
        return along(m, n, zf.at[n], cross)

    def send_near(n):
        return along(m, n, zr.at[n], near)

    def pass_on(f, n):
        return along(beyond if f else cross, n, zw.at[f, n], near)

    def forward(f, n):
        copy = pass_on(f, n)
        copy.wait_recv()
        copy.start()

    def multiply(block, n, bank):
        c_here = lax.broadcasted_iota(jnp.int32, (UNIT, 1), 0) + (w * cl + n * UNIT)
        pair = labels_at(v_starts, c_here) ^ labels_at(v_starts, a_places + block * al)
        for slot in range(slots):
            lane = slot * 2 * al
            value = jnp.concatenate(
                [yb[block, rows_of(n), lane + h * al:lane + (h + 1) * al] for h in range(2)], axis=0)
            for k in range(slot, kt, slots):
                mine = jnp.where(pair == (label_i ^ labels[k]), value, 0.0)
                high = mine.astype(BF16)
                xh[k * UNIT:(k + 1) * UNIT, :al] = high
                xl[k * UNIT:(k + 1) * UNIT, :al] = (mine - high.astype(F32)).astype(BF16)
        right = jnp.concatenate([xh[...], xl[...], xh[...]], axis=0)
        for at in range(0, bj, ROWS):
            high = cth[n, at:at + ROWS, :]
            left = jnp.concatenate([ctl[n, at:at + ROWS, :], high, high], axis=1)
            summed = jnp.dot(left, right, preferred_element_type=F32)
            for x in range(acc.shape[1]):
                before = jnp.where(n > 0, acc[bank, x, at:at + ROWS, :], 0.0)
                acc[bank, x, at:at + ROWS, :] = before + summed[:, x * 128:(x + 1) * 128]

    def members(x):
        if folds == jt:
            return [2 * (x % pairs) + x // pairs]
        if parts == 2:
            x = 2 * (x % 2) + x // 2
        return list(range(x, jt, folds))

    def a_part(ref, t, c):
        if parts == 1:
            return ref.at[t, pl.ds(pairs * c, pairs)]
        if parts == 2:
            return ref.at[t, :, pl.ds(step * c, each)]
        return ref.at[t, pl.ds(c, 1)]

    def b_part(t, p):
        if parts == 1:
            return pk.at[t, pairs * core + p]
        if parts == 2:
            return pk.at[t, p, pl.ds(step * core, each)]
        return pk.at[t, core, pl.ds(step * p, each)]

    def stage_a(t):
        return pltpu.make_async_remote_copy(
            src_ref=a_part(pk, t, 1 - core), dst_ref=ra.at[t], send_sem=sa.at[t], recv_sem=rsa.at[t],
            device_id={"wide": partner}, device_id_type=MESH)

    def stage_b(t, d):
        there = lax.rem(chip + d, pairs)
        return pltpu.make_async_remote_copy(
            src_ref=b_part(t, there), dst_ref=rb.at[t, d - 1], send_sem=sb.at[t, d - 1], recv_sem=rsb.at[t, d - 1],
            device_id={"wide": 2 * there + core}, device_id_type=MESH)

    def target_of(q):
        if parts == 1:
            return w
        if parts == 2:
            return slot_of_chip(chip) + folds * q
        return core + folds * q

    def my_part():
        if parts == 1:
            return 0
        return core if parts == 2 else chip

    def stage_c(t, q, part):
        return pltpu.make_async_remote_copy(
            src_ref=snd.at[t], dst_ref=rc.at[m, part], send_sem=sc.at[t, q], recv_sem=rsc.at[m, part],
            device_id={"wide": target_of(q), "narrow": block_at(t)}, device_id_type=MESH)

    b_labels = labels_at(v_starts, lax.broadcasted_iota(jnp.int32, (bl, 1), 0) + m * bl) ^ label_i
    narrow_places = lax.broadcasted_iota(jnp.int32, (1, 128), 1)
    rest = al - 128
    turns = 128 // rest
    strip = bl // turns

    def pack(t, block, bank):
        pair = [b_labels ^ labels_at(v_starts, narrow_places + (block * al + x * 128)) for x in range(2)]
        for x in range(folds):
            value = []
            for y in range(2):
                total = None
                for j in members(x):
                    here = acc[bank, y, pl.ds(j, bl, stride=jt), :]
                    if parts > 1:
                        here = jnp.where(pair[y] == ir_j[j], here, 0.0 if total is None else total)
                    total = here
                value.append(total)
            whole = bl // 8
            pk[t, x, :whole] = value[0].reshape(whole, 8, 128)
            thin = jnp.concatenate([value[1][q * strip:(q + 1) * strip, :rest] for q in range(turns)], axis=1)
            pk[t, x, whole:] = thin.reshape(strip // 8, 8, 128)
        stage_a(t).start()

    def finish_a(t):
        stage_a(t).wait()
        mine = a_part(pk, t, core)
        mine[...] = mine[...] + ra[t]
        for d in range(1, pairs):
            stage_b(t, d).start()

    def finish_b(t):
        for d in range(1, pairs):
            stage_b(t, d).wait()
        total = b_part(t, chip)[...]
        for d in range(1, pairs):
            total = total + rb[t, d - 1]
        snd[t] = total
        for q in range(parts):
            here = (t == 0) & (target_of(q) == w)

            @pl.when(here)
            def _():
                rc[m, my_part()] = total

            @pl.when(jnp.logical_not(here))
            def _():
                stage_c(t, q, my_part()).start()

    def take_own(n):
        for d in range(1, wn):
            first_copy(n, d).wait()
        joint = kl if slots % kl == 0 else 1
        size = joint * 2 * al
        for slot in range(0, slots, joint):
            total = None
            for k in range(slot, kt, slots):
                lane = k % kl * 2 * al
                part = got[k // kl, rows_of(n), lane:lane + size]
                total = part if total is None else total + part
            yb[m, rows_of(n), slot * 2 * al:slot * 2 * al + size] = total

        @pl.when(inner)
        def _():
            send_cross(n).start()

        @pl.when(outer | (n < 3))
        def _():
            send_near(n).start()

    def after(step, *places):
        chosen = step == STEPS.index(places[0])
        for place in places[1:]:
            chosen = chosen | (step == STEPS.index(place))
        return chosen

    @pl.loop(0, len(STEPS))
    def _(step):
        kind = pick(step, [k for k, _ in STEPS])
        n = pick(step, [c for _, c in STEPS])
        block = block_at(kind)
        bank = jnp.where(kind == 3, 1, 0)

        @pl.when(kind == 0)
        def _():
            take_own(n)

        @pl.when((kind == 3) | (outer & (kind > 0)))
        def _():
            along(block, n, zr.at[n], m).wait_recv()

        multiply(block, n, bank)

        for f, table in enumerate(FORWARD):
            @pl.when(inner & after(step, *table))
            def _():
                forward(f, pick(step, [table.index(p) if p in table else 0 for p in STEPS]))

        @pl.when(outer & after(step, *CROSS))
        def _():
            send_cross(pick(step, [CROSS.index(p) if p in CROSS else 0 for p in STEPS])).start()

        @pl.when(inner & after(step, *NEAR))
        def _():
            send_near(pick(step, [3 + NEAR.index(p) if p in NEAR else 3 for p in STEPS])).start()

        @pl.when(after(step, *PAIRED))
        def _():
            finish_a(pick(step, [PAIRED.index(p) if p in PAIRED else 0 for p in STEPS]))

        @pl.when(after(step, *REDUCED))
        def _():
            finish_b(pick(step, [REDUCED.index(p) if p in REDUCED else 0 for p in STEPS]))

        @pl.when(after(step, *[max((p for p in STEPS if p[0] == k), key=STEPS.index) for k in range(4)]))
        def _():
            pack(kind, block, bank)

    finish_a(nn - 1)
    finish_b(nn - 2)
    finish_b(nn - 1)

    for z in range(nn):
        for u in range(parts):
            @pl.when(jnp.logical_not((m == z) & (owner_of(u) == w)))
            def _():
                pltpu.make_async_remote_copy(
                    src_ref=snd.at[0], dst_ref=rc.at[z, u], send_sem=sc.at[0, 0], recv_sem=rsc.at[z, u],
                    device_id={"wide": partner}, device_id_type=MESH).wait_recv()
    whole = bl // 8
    for z in range(nn):
        done = 0
        thin = []
        for u in range(parts):
            end = step * u + each
            top = min(end, whole)
            if done < top:
                out_t[z * bl + done * 8:z * bl + top * 8, :128] = (
                    rc[z, u, done - step * u:top - step * u].reshape((top - done) * 8, 128))
            low = max(done, whole)
            if low < end:
                thin.append(rc[z, u, low - step * u:end - step * u].reshape((end - low) * 8, 128))
            done = end
        thin = jnp.concatenate(thin, axis=0) if len(thin) > 1 else thin[0]
        for q in range(turns):
            base = z * bl + q * strip
            out_t[base:base + strip, 128:] = thin[:, q * rest:(q + 1) * rest]
    kept = jnp.where(masks_of_own() == (label_i ^ ir_j[w]), out_t[...], 0.0)
    out[...] = jnp.transpose(kept, (1, 0))

    for n in range(chunks):
        send_cross(n).wait_send()
        send_near(n).wait_send()

        @pl.when(inner)
        def _():
            for f in range(2):
                pass_on(f, n).wait_send()
    for t in range(nn):
        for q in range(parts):
            @pl.when((t > 0) | (target_of(q) != w))
            def _():
                stage_c(t, q, my_part()).wait_send()


def packed_path(slots, folds, ident, amps, cycle, irrep_i, irrep_k, irrep_j, irrep_v):
    wn = lax.axis_size("wide")
    nn = lax.axis_size("narrow")
    _, kl, al, vt = amps.shape
    kt, cl, bj = cycle.shape
    bl = bj // wn
    lanes = 2 * kl * al
    chunks = cl // UNIT
    parts = wn // folds
    pairs = wn // 2
    total_tiles, each, _ = tiles_of(bl, al, parts)
    tile = (8, 128)
    first = {1: (pairs, total_tiles), 2: (folds, each), 4: (1, total_tiles)}[parts]
    wide_lanes = -(-al // 256) * 256
    vmem = pl.BlockSpec(memory_space=pltpu.VMEM)
    smem = pl.BlockSpec(memory_space=pltpu.SMEM)
    anywhere = pl.BlockSpec(memory_space=pl.ANY)
    dma = pltpu.SemaphoreType.DMA
    result = pl.pallas_call(
        functools.partial(cycle_kernel, slots, folds, wn, nn),
        out_shape=jax.ShapeDtypeStruct((al, vt), F32),
        in_specs=[anywhere, anywhere, smem, smem, smem, smem],
        out_specs=vmem,
        scratch_shapes=[
            pltpu.VMEM((kl, al, vt), F32),
            pltpu.VMEM((kt, cl, bj), F32),
            pltpu.VMEM((chunks, bj, kt * UNIT), BF16),
            pltpu.VMEM((chunks, bj, kt * UNIT), BF16),
            pltpu.VMEM((wn, cl // 2, lanes), F32),
            pltpu.VMEM((wn, cl // 2, lanes), F32),
            pltpu.VMEM((nn, cl // 2, -(-slots * 2 * al // 128) * 128), F32),
            pltpu.VMEM((kt * UNIT, wide_lanes), BF16),
            pltpu.VMEM((kt * UNIT, wide_lanes), BF16),
            pltpu.VMEM((2, wide_lanes // 128, bj, 128), F32),
            pltpu.VMEM((nn, folds, total_tiles) + tile, F32),
            pltpu.VMEM((nn,) + first + tile, F32),
            pltpu.VMEM((nn, pairs - 1, each) + tile, F32),
            pltpu.VMEM((nn, each) + tile, F32),
            pltpu.VMEM((nn, parts, each) + tile, F32),
            pltpu.VMEM((vt, al), F32),
            dma, dma, dma((chunks, wn)), dma((chunks, wn)), dma((chunks,)), dma((chunks,)),
            dma((2, chunks)), dma((nn, chunks)), dma((nn,)), dma((nn,)), dma((nn, pairs - 1)), dma((nn, pairs - 1)),
            dma((nn, parts)), dma((nn, parts)),
        ],
        compiler_params=pltpu.CompilerParams(
            collective_id=ident, has_side_effects=True, vmem_limit_bytes=56 * 1024 * 1024),
    )(amps[0], cycle, irrep_i, irrep_k, irrep_j, irrep_v)
    return result.reshape(1, 1, al, vt)


def general_path(amps, cycle, irrep_i, irrep_k, irrep_j, irrep_v):
    wide_pos = lax.axis_index("wide")
    narrow_pos = lax.axis_index("narrow")
    wide_count = lax.axis_size("wide")
    narrow_count = lax.axis_size("narrow")
    i_total = amps.shape[0]
    k_local = amps.shape[1]
    a_local = amps.shape[2]
    v_total = amps.shape[3]
    k_total = cycle.shape[0]
    c_local = cycle.shape[1]
    b_local = v_total // narrow_count
    j_total = cycle.shape[2] // b_local
    j_local = j_total // wide_count
    cycle_four = cycle.reshape(k_total, c_local, b_local, j_total)
    k_labels = lax.dynamic_slice_in_dim(irrep_k, wide_pos * k_local, k_local)
    a_labels = lax.dynamic_slice_in_dim(irrep_v, narrow_pos * a_local, a_local)
    allowed_in = (
        irrep_i[:, None, None, None]
        ^ k_labels[None, :, None, None]
        ^ a_labels[None, None, :, None]
        ^ irrep_v[None, None, None, :]
        == 0
    )
    masked = jnp.where(allowed_in, amps, jnp.zeros_like(amps))
    moved = lax.all_to_all(masked, "wide", split_axis=3, concat_axis=1, tiled=True)
    piece = lax.all_gather(moved, "narrow", axis=2, tiled=True)
    part_sum = jnp.einsum("ikac,kcbj->iajb", piece, cycle_four, precision=lax.Precision.HIGHEST)
    terms = part_sum.reshape(piece.shape[0], piece.shape[2], j_total * b_local)
    summed = lax.psum_scatter(terms, "wide", scatter_dimension=2, tiled=True)
    summed_four = summed.reshape(i_total, v_total, j_local, b_local)
    j_labels = lax.dynamic_slice_in_dim(irrep_j, wide_pos * j_local, j_local)
    b_labels = lax.dynamic_slice_in_dim(irrep_v, narrow_pos * b_local, b_local)
    allowed_out = (
        irrep_i[:, None, None, None]
        ^ irrep_v[None, :, None, None]
        ^ j_labels[None, None, :, None]
        ^ b_labels[None, None, None, :]
        == 0
    )
    result = jnp.where(allowed_out, summed_four, jnp.zeros_like(summed_four)).reshape(
        i_total, v_total, j_local * b_local
    )
    returned = lax.all_to_all(result, "narrow", split_axis=1, concat_axis=2, tiled=True)
    spread = returned.reshape(i_total, a_local, narrow_count, j_local, b_local)
    return jnp.transpose(spread, (0, 3, 1, 2, 4)).reshape(i_total, j_local, a_local, v_total)


def level_kernel(labels_k, labels_j, out):
    def larger(labels, size):
        over = jnp.int32(0)
        for k in range(size, labels.shape[0]):
            over = over | jnp.where(labels[k] == labels[k - size], 1, 0)
        return over

    level = jnp.int32(0)
    missed = jnp.int32(1)
    for slots, folds in VARIANTS[:-1]:
        missed = missed & (larger(labels_k, slots) | larger(labels_j, folds))
        level = level + missed
    out[0] = level


def per_device(amps, cycle, irrep_i, irrep_k, irrep_j, irrep_v):
    wn = lax.axis_size("wide")
    nn = lax.axis_size("narrow")
    kt, cl, bj = cycle.shape
    al = amps.shape[2]
    bl = amps.shape[3] // nn
    fits = (amps.shape[0] == 1 and wn == 8 and nn == 4 and bj == bl * wn and bl == al and amps.shape[1] == 2
            and kt == 2 * wn and cl == 5 * UNIT and al == 160 and bj % ROWS == 0)
    if not fits:
        return general_path(amps, cycle, irrep_i, irrep_k, irrep_j, irrep_v)
    smem = pl.BlockSpec(memory_space=pltpu.SMEM)
    level = pl.pallas_call(
        level_kernel,
        out_shape=jax.ShapeDtypeStruct((1,), jnp.int32),
        in_specs=[smem, smem],
        out_specs=smem,
    )(irrep_k, irrep_j)[0]
    paths = [functools.partial(packed_path, *sizes, n) for n, sizes in enumerate(VARIANTS)]
    return lax.switch(level, paths, amps, cycle, irrep_i, irrep_k, irrep_j, irrep_v)


def solution(mesh):
    placed = (P(None, "wide", "narrow", None), P(None, "wide", "narrow"), P(), P(), P(), P())
    return jax.shard_map(
        per_device,
        mesh=mesh,
        in_specs=placed,
        out_specs=P(None, "wide", "narrow", None),
        check_vma=False,
    )
```

```python
import functools

import jax
import jax.numpy as jnp
from jax import lax
from jax.experimental import pallas as pl
from jax.experimental.pallas import tpu as pltpu
from jax.sharding import PartitionSpec as P

F32 = jnp.float32
BF16 = jnp.bfloat16
MESH = pl.DeviceIdType.MESH
UNIT = 16
ROWS = 256
VARIANTS = ((4, 4), (5, 4), (6, 4), (7, 4), (8, 4), (10, 4), (8, 8), (16, 8))
STEPS = ((0, 0), (0, 1), (0, 2), (0, 3), (0, 4), (1, 0), (1, 1), (3, 0), (1, 2), (3, 1), (1, 3), (1, 4),
         (2, 0), (2, 1), (2, 2), (2, 3), (2, 4), (3, 2), (3, 3), (3, 4))
FORWARD = (((0, 2), (0, 3), (0, 4), (1, 0), (1, 1)), ((3, 0), (1, 2), (3, 1), (1, 3), (1, 4)))
CROSS = ((0, 3), (0, 4), (1, 0), (1, 1), (3, 0))
NEAR = ((2, 1), (2, 2))
PAIRED = ((1, 1), (2, 0), (3, 2))
REDUCED = ((2, 1), (3, 2))


def pick(position, table):
    value = jnp.int32(table[0])
    for place in range(1, len(table)):
        if table[place] != table[0]:
            value = jnp.where(position == place, jnp.int32(table[place]), value)
    return value


def run_starts(labels, count):
    steps = count.bit_length()
    starts = []
    for g in range(1, 8):
        low, high = jnp.int32(0), jnp.int32(count)
        for _ in range(steps):
            middle = (low + high) // 2
            below = (labels[jnp.minimum(middle, count - 1)] < g) & (low < high)
            high = jnp.where(below | (low >= high), high, middle)
            low = jnp.where(below, middle + 1, low)
        starts.append(low)
    return starts


def labels_at(starts, places):
    total = jnp.zeros(places.shape, jnp.int32)
    for start in starts:
        total = total + jnp.where(places >= start, 1, 0)
    return total


def tiles_of(bl, al, parts):
    total = bl * al // 1024
    each = -(-total // parts)
    while parts > 1 and (total - each) % (parts - 1):
        each += 1
    return total, each, (total - each) // (parts - 1) if parts > 1 else 0


def cycle_kernel(slots, folds, wn, nn, amps_hbm, cycle, ir_i, ir_k, ir_j, ir_v, out,
                 amps, cyc, cth, ctl, amt, got, yb, xh, xl, acc, pk, ra, rb, snd, rc, out_t,
                 amps_sem, cyc_sem, s1, r1, zr, zf, zw, ry, sa, rsa, sb, rsb, sc, rsc):
    w = lax.axis_index("wide")
    m = lax.axis_index("narrow")
    kl, al, vt = amps.shape
    kt, cl, bj = cyc.shape
    jt = wn
    bl = bj // jt
    chunks = cl // UNIT
    half = UNIT // 2
    parts = jt // folds
    total_tiles, each, step = tiles_of(bl, al, parts)
    pairs = wn // 2
    core = lax.rem(w, 2)
    chip = w // 2
    partner = w + 1 - 2 * core
    inner = (m > 0) & (m < nn - 1)
    outer = jnp.logical_not(inner)
    near = m + 1 - 2 * lax.rem(m, 2)
    low = m < nn // 2
    cross = jnp.where(low, jnp.int32(2), jnp.int32(1))
    beyond = jnp.where(low, jnp.int32(3), jnp.int32(0))

    load_amps = pltpu.make_async_copy(amps_hbm, amps, amps_sem)
    load_amps.start()
    load = pltpu.make_async_copy(cycle, cyc, cyc_sem)

    def slot_of_chip(p):
        return 2 * lax.rem(p, 2) + p // 2

    def owner_of(u):
        if parts == 1:
            return w
        if parts == 2:
            return 2 * slot_of_chip(lax.rem(w, folds)) + u
        return 2 * u + core

    barrier = pltpu.get_barrier_semaphore()
    for d in range(1, wn):
        pl.semaphore_signal(barrier, inc=1, device_id={"wide": lax.rem(w + d, wn)}, device_id_type=MESH)
    for d in range(1, nn):
        pl.semaphore_signal(barrier, inc=1, device_id={"narrow": lax.rem(m + d, nn)}, device_id_type=MESH)
    greeted = wn + nn - 2
    if parts > 1:
        greeted = greeted + parts * (nn - 1)
        for u in range(parts):
            for d in range(1, nn):
                pl.semaphore_signal(barrier, inc=1, device_id={"wide": owner_of(u), "narrow": lax.rem(m + d, nn)},
                                    device_id_type=MESH)

    label_i = ir_i[0]
    labels = [ir_k[k] for k in range(kt)]
    v_starts = run_starts(ir_v, vt)
    a_places = lax.broadcasted_iota(jnp.int32, (1, al), 1)

    def masks_of_own():
        return (labels_at(v_starts, lax.broadcasted_iota(jnp.int32, (vt, 1), 0))
                ^ labels_at(v_starts, a_places + m * al))

    load_amps.wait()
    load.start()
    ca = masks_of_own()
    for e in range(kl):
        turned = jnp.transpose(amps[e], (1, 0))
        kept = jnp.where(ca == (label_i ^ ir_k[w * kl + e]), turned, 0.0)
        for peer in range(wn):
            for n in range(chunks):
                for h in range(2):
                    here = peer * cl + n * UNIT + h * half
                    lane = (2 * e + h) * al
                    amt[peer, n * half:(n + 1) * half, lane:lane + al] = kept[here:here + half]

    pl.semaphore_wait(barrier, greeted)

    def rows_of(n):
        return pl.ds(pl.multiple_of(n * half, half), half)

    def first_copy(n, d):
        return pltpu.make_async_remote_copy(
            src_ref=amt.at[lax.rem(w + d, wn), rows_of(n)], dst_ref=got.at[w, rows_of(n)],
            send_sem=s1.at[n, d], recv_sem=r1.at[n, d], device_id={"wide": lax.rem(w + d, wn)}, device_id_type=MESH)

    for n in range(chunks):
        for d in range(1, wn):
            first_copy(n, d).start()
    got[w] = amt[w]

    if xh.shape[1] > al:
        xh[:, al:] = jnp.zeros((xh.shape[0], xh.shape[1] - al), BF16)
        xl[:, al:] = jnp.zeros((xl.shape[0], xl.shape[1] - al), BF16)
    load.wait()
    ks = 128 // UNIT

    @pl.loop(0, chunks)
    def _(n):
        here = pl.ds(pl.multiple_of(n * UNIT, UNIT), UNIT)
        for g in range(kt // ks):
            for col in range(bj // 128):
                block = cyc[g * ks:(g + 1) * ks, here, col * 128:(col + 1) * 128].reshape(128, 128)
                block = jnp.transpose(block, (1, 0))
                high = block.astype(BF16)
                cth[n, col * 128:(col + 1) * 128, g * 128:(g + 1) * 128] = high
                ctl[n, col * 128:(col + 1) * 128, g * 128:(g + 1) * 128] = (block - high.astype(F32)).astype(BF16)

    def block_at(t):
        return jnp.where(t == 0, m, jnp.where(t == 1, cross, jnp.where(t == 2, beyond, near)))

    def along(block, n, sem, target):
        return pltpu.make_async_remote_copy(
            src_ref=yb.at[block, rows_of(n)], dst_ref=yb.at[block, rows_of(n)], send_sem=sem,
            recv_sem=ry.at[block, n], device_id={"narrow": target}, device_id_type=MESH)

    def send_cross(n):
        return along(m, n, zf.at[n], cross)

    def send_near(n):
        return along(m, n, zr.at[n], near)

    def pass_on(f, n):
        return along(beyond if f else cross, n, zw.at[f, n], near)

    def forward(f, n):
        copy = pass_on(f, n)
        copy.wait_recv()
        copy.start()

    def multiply(block, n, bank):
        c_here = lax.broadcasted_iota(jnp.int32, (UNIT, 1), 0) + (w * cl + n * UNIT)
        pair = labels_at(v_starts, c_here) ^ labels_at(v_starts, a_places + block * al)
        for slot in range(slots):
            lane = slot * 2 * al
            value = jnp.concatenate(
                [yb[block, rows_of(n), lane + h * al:lane + (h + 1) * al] for h in range(2)], axis=0)
            for k in range(slot, kt, slots):
                mine = jnp.where(pair == (label_i ^ labels[k]), value, 0.0)
                high = mine.astype(BF16)
                xh[k * UNIT:(k + 1) * UNIT, :al] = high
                xl[k * UNIT:(k + 1) * UNIT, :al] = (mine - high.astype(F32)).astype(BF16)
        right = jnp.concatenate([xh[...], xl[...], xh[...]], axis=0)
        for at in range(0, bj, ROWS):
            high = cth[n, at:at + ROWS, :]
            left = jnp.concatenate([ctl[n, at:at + ROWS, :], high, high], axis=1)
            summed = jnp.dot(left, right, preferred_element_type=F32)
            for x in range(acc.shape[1]):
                before = jnp.where(n > 0, acc[bank, x, at:at + ROWS, :], 0.0)
                acc[bank, x, at:at + ROWS, :] = before + summed[:, x * 128:(x + 1) * 128]

    def members(x):
        if folds == jt:
            return [2 * (x % pairs) + x // pairs]
        if parts == 2:
            x = 2 * (x % 2) + x // 2
        return list(range(x, jt, folds))

    def a_part(ref, t, c):
        if parts == 1:
            return ref.at[t, pl.ds(pairs * c, pairs)]
        if parts == 2:
            return ref.at[t, :, pl.ds(step * c, each)]
        return ref.at[t, pl.ds(c, 1)]

    def b_part(t, p):
        if parts == 1:
            return pk.at[t, pairs * core + p]
        if parts == 2:
            return pk.at[t, p, pl.ds(step * core, each)]
        return pk.at[t, core, pl.ds(step * p, each)]

    def stage_a(t):
        return pltpu.make_async_remote_copy(
            src_ref=a_part(pk, t, 1 - core), dst_ref=ra.at[t], send_sem=sa.at[t], recv_sem=rsa.at[t],
            device_id={"wide": partner}, device_id_type=MESH)

    def stage_b(t, d):
        there = lax.rem(chip + d, pairs)
        return pltpu.make_async_remote_copy(
            src_ref=b_part(t, there), dst_ref=rb.at[t, d - 1], send_sem=sb.at[t, d - 1], recv_sem=rsb.at[t, d - 1],
            device_id={"wide": 2 * there + core}, device_id_type=MESH)

    def target_of(q):
        if parts == 1:
            return w
        if parts == 2:
            return slot_of_chip(chip) + folds * q
        return core + folds * q

    def my_part():
        if parts == 1:
            return 0
        return core if parts == 2 else chip

    def stage_c(t, q, part):
        return pltpu.make_async_remote_copy(
            src_ref=snd.at[t], dst_ref=rc.at[m, part], send_sem=sc.at[t, q], recv_sem=rsc.at[m, part],
            device_id={"wide": target_of(q), "narrow": block_at(t)}, device_id_type=MESH)

    b_labels = labels_at(v_starts, lax.broadcasted_iota(jnp.int32, (bl, 1), 0) + m * bl) ^ label_i
    narrow_places = lax.broadcasted_iota(jnp.int32, (1, 128), 1)
    rest = al - 128
    turns = 128 // rest
    strip = bl // turns

    def pack(t, block, bank):
        pair = [b_labels ^ labels_at(v_starts, narrow_places + (block * al + x * 128)) for x in range(2)]
        for x in range(folds):
            value = []
            for y in range(2):
                total = None
                for j in members(x):
                    here = acc[bank, y, pl.ds(j, bl, stride=jt), :]
                    if parts > 1:
                        here = jnp.where(pair[y] == ir_j[j], here, 0.0 if total is None else total)
                    total = here
                value.append(total)
            whole = bl // 8
            pk[t, x, :whole] = value[0].reshape(whole, 8, 128)
            thin = jnp.concatenate([value[1][q * strip:(q + 1) * strip, :rest] for q in range(turns)], axis=1)
            pk[t, x, whole:] = thin.reshape(strip // 8, 8, 128)
        stage_a(t).start()

    def finish_a(t):
        stage_a(t).wait()
        mine = a_part(pk, t, core)
        mine[...] = mine[...] + ra[t]
        for d in range(1, pairs):
            stage_b(t, d).start()

    def finish_b(t):
        for d in range(1, pairs):
            stage_b(t, d).wait()
        total = b_part(t, chip)[...]
        for d in range(1, pairs):
            total = total + rb[t, d - 1]
        snd[t] = total
        for q in range(parts):
            here = (t == 0) & (target_of(q) == w)

            @pl.when(here)
            def _():
                rc[m, my_part()] = total

            @pl.when(jnp.logical_not(here))
            def _():
                stage_c(t, q, my_part()).start()

    def take_own(n):
        for d in range(1, wn):
            first_copy(n, d).wait()
        joint = kl if slots % kl == 0 else 1
        size = joint * 2 * al
        for slot in range(0, slots, joint):
            total = None
            for k in range(slot, kt, slots):
                lane = k % kl * 2 * al
                part = got[k // kl, rows_of(n), lane:lane + size]
                total = part if total is None else total + part
            yb[m, rows_of(n), slot * 2 * al:slot * 2 * al + size] = total

        @pl.when(inner)
        def _():
            send_cross(n).start()

        @pl.when(outer | (n < 3))
        def _():
            send_near(n).start()

    def after(step, *places):
        chosen = step == STEPS.index(places[0])
        for place in places[1:]:
            chosen = chosen | (step == STEPS.index(place))
        return chosen

    @pl.loop(0, len(STEPS))
    def _(step):
        kind = pick(step, [k for k, _ in STEPS])
        n = pick(step, [c for _, c in STEPS])
        block = block_at(kind)
        bank = jnp.where(kind == 3, 1, 0)

        @pl.when(kind == 0)
        def _():
            take_own(n)

        @pl.when((kind == 3) | (outer & (kind > 0)))
        def _():
            along(block, n, zr.at[n], m).wait_recv()

        multiply(block, n, bank)

        for f, table in enumerate(FORWARD):
            @pl.when(inner & after(step, *table))
            def _():
                forward(f, pick(step, [table.index(p) if p in table else 0 for p in STEPS]))

        @pl.when(outer & after(step, *CROSS))
        def _():
            send_cross(pick(step, [CROSS.index(p) if p in CROSS else 0 for p in STEPS])).start()

        @pl.when(inner & after(step, *NEAR))
        def _():
            send_near(pick(step, [3 + NEAR.index(p) if p in NEAR else 3 for p in STEPS])).start()

        @pl.when(after(step, *PAIRED))
        def _():
            finish_a(pick(step, [PAIRED.index(p) if p in PAIRED else 0 for p in STEPS]))

        @pl.when(after(step, *REDUCED))
        def _():
            finish_b(pick(step, [REDUCED.index(p) if p in REDUCED else 0 for p in STEPS]))

        @pl.when(after(step, *[max((p for p in STEPS if p[0] == k), key=STEPS.index) for k in range(4)]))
        def _():
            pack(kind, block, bank)

    finish_a(nn - 1)
    finish_b(nn - 2)
    finish_b(nn - 1)

    for z in range(nn):
        for u in range(parts):
            @pl.when(jnp.logical_not((m == z) & (owner_of(u) == w)))
            def _():
                pltpu.make_async_remote_copy(
                    src_ref=snd.at[0], dst_ref=rc.at[z, u], send_sem=sc.at[0, 0], recv_sem=rsc.at[z, u],
                    device_id={"wide": partner}, device_id_type=MESH).wait_recv()
    whole = bl // 8
    for z in range(nn):
        done = 0
        thin = []
        for u in range(parts):
            end = step * u + each
            top = min(end, whole)
            if done < top:
                out_t[z * bl + done * 8:z * bl + top * 8, :128] = (
                    rc[z, u, done - step * u:top - step * u].reshape((top - done) * 8, 128))
            low = max(done, whole)
            if low < end:
                thin.append(rc[z, u, low - step * u:end - step * u].reshape((end - low) * 8, 128))
            done = end
        thin = jnp.concatenate(thin, axis=0) if len(thin) > 1 else thin[0]
        for q in range(turns):
            base = z * bl + q * strip
            out_t[base:base + strip, 128:] = thin[:, q * rest:(q + 1) * rest]
    kept = jnp.where(masks_of_own() == (label_i ^ ir_j[w]), out_t[...], 0.0)
    out[...] = jnp.transpose(kept, (1, 0))

    for n in range(chunks):
        send_cross(n).wait_send()
        send_near(n).wait_send()

        @pl.when(inner)
        def _():
            for f in range(2):
                pass_on(f, n).wait_send()
    for t in range(nn):
        for q in range(parts):
            @pl.when((t > 0) | (target_of(q) != w))
            def _():
                stage_c(t, q, my_part()).wait_send()


def packed_path(slots, folds, ident, amps, cycle, irrep_i, irrep_k, irrep_j, irrep_v):
    wn = lax.axis_size("wide")
    nn = lax.axis_size("narrow")
    _, kl, al, vt = amps.shape
    kt, cl, bj = cycle.shape
    bl = bj // wn
    lanes = 2 * kl * al
    chunks = cl // UNIT
    parts = wn // folds
    pairs = wn // 2
    total_tiles, each, _ = tiles_of(bl, al, parts)
    tile = (8, 128)
    first = {1: (pairs, total_tiles), 2: (folds, each), 4: (1, total_tiles)}[parts]
    wide_lanes = -(-al // 256) * 256
    vmem = pl.BlockSpec(memory_space=pltpu.VMEM)
    smem = pl.BlockSpec(memory_space=pltpu.SMEM)
    anywhere = pl.BlockSpec(memory_space=pl.ANY)
    dma = pltpu.SemaphoreType.DMA
    result = pl.pallas_call(
        functools.partial(cycle_kernel, slots, folds, wn, nn),
        out_shape=jax.ShapeDtypeStruct((al, vt), F32),
        in_specs=[anywhere, anywhere, smem, smem, smem, smem],
        out_specs=vmem,
        scratch_shapes=[
            pltpu.VMEM((kl, al, vt), F32),
            pltpu.VMEM((kt, cl, bj), F32),
            pltpu.VMEM((chunks, bj, kt * UNIT), BF16),
            pltpu.VMEM((chunks, bj, kt * UNIT), BF16),
            pltpu.VMEM((wn, cl // 2, lanes), F32),
            pltpu.VMEM((wn, cl // 2, lanes), F32),
            pltpu.VMEM((nn, cl // 2, -(-slots * 2 * al // 128) * 128), F32),
            pltpu.VMEM((kt * UNIT, wide_lanes), BF16),
            pltpu.VMEM((kt * UNIT, wide_lanes), BF16),
            pltpu.VMEM((2, wide_lanes // 128, bj, 128), F32),
            pltpu.VMEM((nn, folds, total_tiles) + tile, F32),
            pltpu.VMEM((nn,) + first + tile, F32),
            pltpu.VMEM((nn, pairs - 1, each) + tile, F32),
            pltpu.VMEM((nn, each) + tile, F32),
            pltpu.VMEM((nn, parts, each) + tile, F32),
            pltpu.VMEM((vt, al), F32),
            dma, dma, dma((chunks, wn)), dma((chunks, wn)), dma((chunks,)), dma((chunks,)),
            dma((2, chunks)), dma((nn, chunks)), dma((nn,)), dma((nn,)), dma((nn, pairs - 1)), dma((nn, pairs - 1)),
            dma((nn, parts)), dma((nn, parts)),
        ],
        compiler_params=pltpu.CompilerParams(
            collective_id=ident, has_side_effects=True, vmem_limit_bytes=56 * 1024 * 1024),
    )(amps[0], cycle, irrep_i, irrep_k, irrep_j, irrep_v)
    return result.reshape(1, 1, al, vt)


def general_path(amps, cycle, irrep_i, irrep_k, irrep_j, irrep_v):
    wide_pos = lax.axis_index("wide")
    narrow_pos = lax.axis_index("narrow")
    wide_count = lax.axis_size("wide")
    narrow_count = lax.axis_size("narrow")
    i_total = amps.shape[0]
    k_local = amps.shape[1]
    a_local = amps.shape[2]
    v_total = amps.shape[3]
    k_total = cycle.shape[0]
    c_local = cycle.shape[1]
    b_local = v_total // narrow_count
    j_total = cycle.shape[2] // b_local
    j_local = j_total // wide_count
    cycle_four = cycle.reshape(k_total, c_local, b_local, j_total)
    k_labels = lax.dynamic_slice_in_dim(irrep_k, wide_pos * k_local, k_local)
    a_labels = lax.dynamic_slice_in_dim(irrep_v, narrow_pos * a_local, a_local)
    allowed_in = (
        irrep_i[:, None, None, None]
        ^ k_labels[None, :, None, None]
        ^ a_labels[None, None, :, None]
        ^ irrep_v[None, None, None, :]
        == 0
    )
    masked = jnp.where(allowed_in, amps, jnp.zeros_like(amps))
    moved = lax.all_to_all(masked, "wide", split_axis=3, concat_axis=1, tiled=True)
    piece = lax.all_gather(moved, "narrow", axis=2, tiled=True)
    part_sum = jnp.einsum("ikac,kcbj->iajb", piece, cycle_four, precision=lax.Precision.HIGHEST)
    terms = part_sum.reshape(piece.shape[0], piece.shape[2], j_total * b_local)
    summed = lax.psum_scatter(terms, "wide", scatter_dimension=2, tiled=True)
    summed_four = summed.reshape(i_total, v_total, j_local, b_local)
    j_labels = lax.dynamic_slice_in_dim(irrep_j, wide_pos * j_local, j_local)
    b_labels = lax.dynamic_slice_in_dim(irrep_v, narrow_pos * b_local, b_local)
    allowed_out = (
        irrep_i[:, None, None, None]
        ^ irrep_v[None, :, None, None]
        ^ j_labels[None, None, :, None]
        ^ b_labels[None, None, None, :]
        == 0
    )
    result = jnp.where(allowed_out, summed_four, jnp.zeros_like(summed_four)).reshape(
        i_total, v_total, j_local * b_local
    )
    returned = lax.all_to_all(result, "narrow", split_axis=1, concat_axis=2, tiled=True)
    spread = returned.reshape(i_total, a_local, narrow_count, j_local, b_local)
    return jnp.transpose(spread, (0, 3, 1, 2, 4)).reshape(i_total, j_local, a_local, v_total)


def level_kernel(labels_k, labels_j, out):
    def larger(labels, size):
        over = jnp.int32(0)
        for k in range(size, labels.shape[0]):
            over = over | jnp.where(labels[k] == labels[k - size], 1, 0)
        return over

    level = jnp.int32(0)
    missed = jnp.int32(1)
    for slots, folds in VARIANTS[:-1]:
        missed = missed & (larger(labels_k, slots) | larger(labels_j, folds))
        level = level + missed
    out[0] = level


def per_device(amps, cycle, irrep_i, irrep_k, irrep_j, irrep_v):
    wn = lax.axis_size("wide")
    nn = lax.axis_size("narrow")
    kt, cl, bj = cycle.shape
    al = amps.shape[2]
    bl = amps.shape[3] // nn
    fits = (amps.shape[0] == 1 and wn == 8 and nn == 4 and bj == bl * wn and bl == al and amps.shape[1] == 2
            and kt == 2 * wn and cl == 5 * UNIT and al == 160 and bj % ROWS == 0)
    if not fits:
        return general_path(amps, cycle, irrep_i, irrep_k, irrep_j, irrep_v)
    smem = pl.BlockSpec(memory_space=pltpu.SMEM)
    level = pl.pallas_call(
        level_kernel,
        out_shape=jax.ShapeDtypeStruct((1,), jnp.int32),
        in_specs=[smem, smem],
        out_specs=smem,
    )(irrep_k, irrep_j)[0]
    paths = [functools.partial(packed_path, *sizes, n) for n, sizes in enumerate(VARIANTS)]
    return lax.switch(level, paths, amps, cycle, irrep_i, irrep_k, irrep_j, irrep_v)


def solution(mesh):
    placed = (P(None, "wide", "narrow", None), P(None, "wide", "narrow"), P(), P(), P(), P())
    return jax.shard_map(
        per_device,
        mesh=mesh,
        in_specs=placed,
        out_specs=P(None, "wide", "narrow", None),
        check_vma=False,
    )
```

```python
import functools

import jax
import jax.numpy as jnp
from jax import lax
from jax.experimental import pallas as pl
from jax.experimental.pallas import tpu as pltpu
from jax.sharding import PartitionSpec as P

F32 = jnp.float32
BF16 = jnp.bfloat16
MESH = pl.DeviceIdType.MESH
UNIT = 16
ROWS = 256
VARIANTS = ((4, 4), (5, 4), (6, 4), (7, 4), (8, 4), (10, 4), (8, 8), (16, 8))
STEPS = ((0, 0), (0, 1), (0, 2), (0, 3), (0, 4), (1, 0), (1, 1), (3, 0), (1, 2), (3, 1), (1, 3), (1, 4),
         (2, 0), (2, 1), (2, 2), (2, 3), (2, 4), (3, 2), (3, 3), (3, 4))
FORWARD = (((0, 2), (0, 3), (0, 4), (1, 0), (1, 1)), ((3, 0), (1, 2), (3, 1), (1, 3), (1, 4)))
CROSS = ((0, 3), (0, 4), (1, 0), (1, 1), (3, 0))
NEAR = ((2, 1), (2, 2))
PAIRED = ((1, 1), (2, 0), (3, 2))
REDUCED = ((2, 1), (2, 4))


def pick(position, table):
    value = jnp.int32(table[0])
    for place in range(1, len(table)):
        if table[place] != table[0]:
            value = jnp.where(position == place, jnp.int32(table[place]), value)
    return value


def run_starts(labels, count):
    steps = count.bit_length()
    starts = []
    for g in range(1, 8):
        low, high = jnp.int32(0), jnp.int32(count)
        for _ in range(steps):
            middle = (low + high) // 2
            below = (labels[jnp.minimum(middle, count - 1)] < g) & (low < high)
            high = jnp.where(below | (low >= high), high, middle)
            low = jnp.where(below, middle + 1, low)
        starts.append(low)
    return starts


def labels_at(starts, places):
    total = jnp.zeros(places.shape, jnp.int32)
    for start in starts:
        total = total + jnp.where(places >= start, 1, 0)
    return total


def tiles_of(bl, al, parts):
    total = bl * al // 1024
    each = -(-total // parts)
    while parts > 1 and (total - each) % (parts - 1):
        each += 1
    return total, each, (total - each) // (parts - 1) if parts > 1 else 0


def cycle_kernel(slots, folds, wn, nn, amps_hbm, cycle, ir_i, ir_k, ir_j, ir_v, out,
                 amps, cyc, cth, ctl, amt, got, yb, xh, xl, acc, pk, ra, rb, snd, rc, out_t,
                 amps_sem, cyc_sem, s1, r1, zr, zf, zw, ry, sa, rsa, sb, rsb, sc, rsc):
    w = lax.axis_index("wide")
    m = lax.axis_index("narrow")
    kl, al, vt = amps.shape
    kt, cl, bj = cyc.shape
    jt = wn
    bl = bj // jt
    chunks = cl // UNIT
    half = UNIT // 2
    parts = jt // folds
    total_tiles, each, step = tiles_of(bl, al, parts)
    pairs = wn // 2
    core = lax.rem(w, 2)
    chip = w // 2
    partner = w + 1 - 2 * core
    inner = (m > 0) & (m < nn - 1)
    outer = jnp.logical_not(inner)
    near = m + 1 - 2 * lax.rem(m, 2)
    low = m < nn // 2
    cross = jnp.where(low, jnp.int32(2), jnp.int32(1))
    beyond = jnp.where(low, jnp.int32(3), jnp.int32(0))

    load_amps = pltpu.make_async_copy(amps_hbm, amps, amps_sem)
    load_amps.start()
    load = pltpu.make_async_copy(cycle, cyc, cyc_sem)

    def slot_of_chip(p):
        return 2 * lax.rem(p, 2) + p // 2

    def owner_of(u):
        if parts == 1:
            return w
        if parts == 2:
            return 2 * slot_of_chip(lax.rem(w, folds)) + u
        return 2 * u + core

    barrier = pltpu.get_barrier_semaphore()
    for d in range(1, wn):
        pl.semaphore_signal(barrier, inc=1, device_id={"wide": lax.rem(w + d, wn)}, device_id_type=MESH)
    for d in range(1, nn):
        pl.semaphore_signal(barrier, inc=1, device_id={"narrow": lax.rem(m + d, nn)}, device_id_type=MESH)
    greeted = wn + nn - 2
    if parts > 1:
        greeted = greeted + parts * (nn - 1)
        for u in range(parts):
            for d in range(1, nn):
                pl.semaphore_signal(barrier, inc=1, device_id={"wide": owner_of(u), "narrow": lax.rem(m + d, nn)},
                                    device_id_type=MESH)

    label_i = ir_i[0]
    labels = [ir_k[k] for k in range(kt)]
    v_starts = run_starts(ir_v, vt)
    a_places = lax.broadcasted_iota(jnp.int32, (1, al), 1)

    def masks_of_own():
        return (labels_at(v_starts, lax.broadcasted_iota(jnp.int32, (vt, 1), 0))
                ^ labels_at(v_starts, a_places + m * al))

    load_amps.wait()
    load.start()
    ca = masks_of_own()
    for e in range(kl):
        turned = jnp.transpose(amps[e], (1, 0))
        kept = jnp.where(ca == (label_i ^ ir_k[w * kl + e]), turned, 0.0)
        for peer in range(wn):
            for n in range(chunks):
                for h in range(2):
                    here = peer * cl + n * UNIT + h * half
                    lane = (2 * e + h) * al
                    amt[peer, n * half:(n + 1) * half, lane:lane + al] = kept[here:here + half]

    pl.semaphore_wait(barrier, greeted)

    def rows_of(n):
        return pl.ds(pl.multiple_of(n * half, half), half)

    def first_copy(n, d):
        return pltpu.make_async_remote_copy(
            src_ref=amt.at[lax.rem(w + d, wn), rows_of(n)], dst_ref=got.at[w, rows_of(n)],
            send_sem=s1.at[n, d], recv_sem=r1.at[n, d], device_id={"wide": lax.rem(w + d, wn)}, device_id_type=MESH)

    for n in range(chunks):
        for d in range(1, wn):
            first_copy(n, d).start()
    got[w] = amt[w]

    if xh.shape[1] > al:
        xh[:, al:] = jnp.zeros((xh.shape[0], xh.shape[1] - al), BF16)
        xl[:, al:] = jnp.zeros((xl.shape[0], xl.shape[1] - al), BF16)
    load.wait()
    ks = 128 // UNIT

    @pl.loop(0, chunks)
    def _(n):
        here = pl.ds(pl.multiple_of(n * UNIT, UNIT), UNIT)
        for g in range(kt // ks):
            for col in range(bj // 128):
                block = cyc[g * ks:(g + 1) * ks, here, col * 128:(col + 1) * 128].reshape(128, 128)
                block = jnp.transpose(block, (1, 0))
                high = block.astype(BF16)
                cth[n, col * 128:(col + 1) * 128, g * 128:(g + 1) * 128] = high
                ctl[n, col * 128:(col + 1) * 128, g * 128:(g + 1) * 128] = (block - high.astype(F32)).astype(BF16)

    def block_at(t):
        return jnp.where(t == 0, m, jnp.where(t == 1, cross, jnp.where(t == 2, beyond, near)))

    def along(block, n, sem, target):
        return pltpu.make_async_remote_copy(
            src_ref=yb.at[block, rows_of(n)], dst_ref=yb.at[block, rows_of(n)], send_sem=sem,
            recv_sem=ry.at[block, n], device_id={"narrow": target}, device_id_type=MESH)

    def send_cross(n):
        return along(m, n, zf.at[n], cross)

    def send_near(n):
        return along(m, n, zr.at[n], near)

    def pass_on(f, n):
        return along(beyond if f else cross, n, zw.at[f, n], near)

    def forward(f, n):
        copy = pass_on(f, n)
        copy.wait_recv()
        copy.start()

    def multiply(block, n, bank):
        c_here = lax.broadcasted_iota(jnp.int32, (UNIT, 1), 0) + (w * cl + n * UNIT)
        pair = labels_at(v_starts, c_here) ^ labels_at(v_starts, a_places + block * al)
        for slot in range(slots):
            lane = slot * 2 * al
            value = jnp.concatenate(
                [yb[block, rows_of(n), lane + h * al:lane + (h + 1) * al] for h in range(2)], axis=0)
            for k in range(slot, kt, slots):
                mine = jnp.where(pair == (label_i ^ labels[k]), value, 0.0)
                high = mine.astype(BF16)
                xh[k * UNIT:(k + 1) * UNIT, :al] = high
                xl[k * UNIT:(k + 1) * UNIT, :al] = (mine - high.astype(F32)).astype(BF16)
        right = jnp.concatenate([xh[...], xl[...], xh[...]], axis=0)
        for at in range(0, bj, ROWS):
            high = cth[n, at:at + ROWS, :]
            left = jnp.concatenate([ctl[n, at:at + ROWS, :], high, high], axis=1)
            summed = jnp.dot(left, right, preferred_element_type=F32)
            for x in range(acc.shape[1]):
                before = jnp.where(n > 0, acc[bank, x, at:at + ROWS, :], 0.0)
                acc[bank, x, at:at + ROWS, :] = before + summed[:, x * 128:(x + 1) * 128]

    def members(x):
        if folds == jt:
            return [2 * (x % pairs) + x // pairs]
        if parts == 2:
            x = 2 * (x % 2) + x // 2
        return list(range(x, jt, folds))

    def a_part(ref, t, c):
        if parts == 1:
            return ref.at[t, pl.ds(pairs * c, pairs)]
        if parts == 2:
            return ref.at[t, :, pl.ds(step * c, each)]
        return ref.at[t, pl.ds(c, 1)]

    def b_part(t, p):
        if parts == 1:
            return pk.at[t, pairs * core + p]
        if parts == 2:
            return pk.at[t, p, pl.ds(step * core, each)]
        return pk.at[t, core, pl.ds(step * p, each)]

    def stage_a(t):
        return pltpu.make_async_remote_copy(
            src_ref=a_part(pk, t, 1 - core), dst_ref=ra.at[t], send_sem=sa.at[t], recv_sem=rsa.at[t],
            device_id={"wide": partner}, device_id_type=MESH)

    def stage_b(t, d):
        there = lax.rem(chip + d, pairs)
        return pltpu.make_async_remote_copy(
            src_ref=b_part(t, there), dst_ref=rb.at[t, d - 1], send_sem=sb.at[t, d - 1], recv_sem=rsb.at[t, d - 1],
            device_id={"wide": 2 * there + core}, device_id_type=MESH)

    def target_of(q):
        if parts == 1:
            return w
        if parts == 2:
            return slot_of_chip(chip) + folds * q
        return core + folds * q

    def my_part():
        if parts == 1:
            return 0
        return core if parts == 2 else chip

    def stage_c(t, q, part):
        return pltpu.make_async_remote_copy(
            src_ref=snd.at[t], dst_ref=rc.at[m, part], send_sem=sc.at[t, q], recv_sem=rsc.at[m, part],
            device_id={"wide": target_of(q), "narrow": block_at(t)}, device_id_type=MESH)

    b_labels = labels_at(v_starts, lax.broadcasted_iota(jnp.int32, (bl, 1), 0) + m * bl) ^ label_i
    narrow_places = lax.broadcasted_iota(jnp.int32, (1, 128), 1)
    rest = al - 128
    turns = 128 // rest
    strip = bl // turns

    def pack(t, block, bank):
        pair = [b_labels ^ labels_at(v_starts, narrow_places + (block * al + x * 128)) for x in range(2)]
        for x in range(folds):
            value = []
            for y in range(2):
                total = None
                for j in members(x):
                    here = acc[bank, y, pl.ds(j, bl, stride=jt), :]
                    if parts > 1:
                        here = jnp.where(pair[y] == ir_j[j], here, 0.0 if total is None else total)
                    total = here
                value.append(total)
            whole = bl // 8
            pk[t, x, :whole] = value[0].reshape(whole, 8, 128)
            thin = jnp.concatenate([value[1][q * strip:(q + 1) * strip, :rest] for q in range(turns)], axis=1)
            pk[t, x, whole:] = thin.reshape(strip // 8, 8, 128)
        stage_a(t).start()

    def finish_a(t):
        stage_a(t).wait()
        mine = a_part(pk, t, core)
        mine[...] = mine[...] + ra[t]
        for d in range(1, pairs):
            stage_b(t, d).start()

    def finish_b(t):
        for d in range(1, pairs):
            stage_b(t, d).wait()
        total = b_part(t, chip)[...]
        for d in range(1, pairs):
            total = total + rb[t, d - 1]
        snd[t] = total
        for q in range(parts):
            here = (t == 0) & (target_of(q) == w)

            @pl.when(here)
            def _():
                rc[m, my_part()] = total

            @pl.when(jnp.logical_not(here))
            def _():
                stage_c(t, q, my_part()).start()

    def take_own(n):
        for d in range(1, wn):
            first_copy(n, d).wait()
        joint = kl if slots % kl == 0 else 1
        size = joint * 2 * al
        for slot in range(0, slots, joint):
            total = None
            for k in range(slot, kt, slots):
                lane = k % kl * 2 * al
                part = got[k // kl, rows_of(n), lane:lane + size]
                total = part if total is None else total + part
            yb[m, rows_of(n), slot * 2 * al:slot * 2 * al + size] = total

        @pl.when(inner)
        def _():
            send_cross(n).start()

        @pl.when(outer | (n < 3))
        def _():
            send_near(n).start()

    def after(step, *places):
        chosen = step == STEPS.index(places[0])
        for place in places[1:]:
            chosen = chosen | (step == STEPS.index(place))
        return chosen

    @pl.loop(0, len(STEPS))
    def _(step):
        kind = pick(step, [k for k, _ in STEPS])
        n = pick(step, [c for _, c in STEPS])
        block = block_at(kind)
        bank = jnp.where(kind == 3, 1, 0)

        @pl.when(kind == 0)
        def _():
            take_own(n)

        @pl.when((kind == 3) | (outer & (kind > 0)))
        def _():
            along(block, n, zr.at[n], m).wait_recv()

        multiply(block, n, bank)

        for f, table in enumerate(FORWARD):
            @pl.when(inner & after(step, *table))
            def _():
                forward(f, pick(step, [table.index(p) if p in table else 0 for p in STEPS]))

        @pl.when(outer & after(step, *CROSS))
        def _():
            send_cross(pick(step, [CROSS.index(p) if p in CROSS else 0 for p in STEPS])).start()

        @pl.when(inner & after(step, *NEAR))
        def _():
            send_near(pick(step, [3 + NEAR.index(p) if p in NEAR else 3 for p in STEPS])).start()

        @pl.when(after(step, *PAIRED))
        def _():
            finish_a(pick(step, [PAIRED.index(p) if p in PAIRED else 0 for p in STEPS]))

        @pl.when(after(step, *REDUCED))
        def _():
            finish_b(pick(step, [REDUCED.index(p) if p in REDUCED else 0 for p in STEPS]))

        @pl.when(after(step, *[max((p for p in STEPS if p[0] == k), key=STEPS.index) for k in range(4)]))
        def _():
            pack(kind, block, bank)

    finish_a(nn - 1)
    finish_b(nn - 2)
    finish_b(nn - 1)

    for z in range(nn):
        for u in range(parts):
            @pl.when(jnp.logical_not((m == z) & (owner_of(u) == w)))
            def _():
                pltpu.make_async_remote_copy(
                    src_ref=snd.at[0], dst_ref=rc.at[z, u], send_sem=sc.at[0, 0], recv_sem=rsc.at[z, u],
                    device_id={"wide": partner}, device_id_type=MESH).wait_recv()
    whole = bl // 8
    for z in range(nn):
        done = 0
        thin = []
        for u in range(parts):
            end = step * u + each
            top = min(end, whole)
            if done < top:
                out_t[z * bl + done * 8:z * bl + top * 8, :128] = (
                    rc[z, u, done - step * u:top - step * u].reshape((top - done) * 8, 128))
            low = max(done, whole)
            if low < end:
                thin.append(rc[z, u, low - step * u:end - step * u].reshape((end - low) * 8, 128))
            done = end
        thin = jnp.concatenate(thin, axis=0) if len(thin) > 1 else thin[0]
        for q in range(turns):
            base = z * bl + q * strip
            out_t[base:base + strip, 128:] = thin[:, q * rest:(q + 1) * rest]
    kept = jnp.where(masks_of_own() == (label_i ^ ir_j[w]), out_t[...], 0.0)
    out[...] = jnp.transpose(kept, (1, 0))

    for n in range(chunks):
        send_cross(n).wait_send()
        send_near(n).wait_send()

        @pl.when(inner)
        def _():
            for f in range(2):
                pass_on(f, n).wait_send()
    for t in range(nn):
        for q in range(parts):
            @pl.when((t > 0) | (target_of(q) != w))
            def _():
                stage_c(t, q, my_part()).wait_send()


def packed_path(slots, folds, ident, amps, cycle, irrep_i, irrep_k, irrep_j, irrep_v):
    wn = lax.axis_size("wide")
    nn = lax.axis_size("narrow")
    _, kl, al, vt = amps.shape
    kt, cl, bj = cycle.shape
    bl = bj // wn
    lanes = 2 * kl * al
    chunks = cl // UNIT
    parts = wn // folds
    pairs = wn // 2
    total_tiles, each, _ = tiles_of(bl, al, parts)
    tile = (8, 128)
    first = {1: (pairs, total_tiles), 2: (folds, each), 4: (1, total_tiles)}[parts]
    wide_lanes = -(-al // 256) * 256
    vmem = pl.BlockSpec(memory_space=pltpu.VMEM)
    smem = pl.BlockSpec(memory_space=pltpu.SMEM)
    anywhere = pl.BlockSpec(memory_space=pl.ANY)
    dma = pltpu.SemaphoreType.DMA
    result = pl.pallas_call(
        functools.partial(cycle_kernel, slots, folds, wn, nn),
        out_shape=jax.ShapeDtypeStruct((al, vt), F32),
        in_specs=[anywhere, anywhere, smem, smem, smem, smem],
        out_specs=vmem,
        scratch_shapes=[
            pltpu.VMEM((kl, al, vt), F32),
            pltpu.VMEM((kt, cl, bj), F32),
            pltpu.VMEM((chunks, bj, kt * UNIT), BF16),
            pltpu.VMEM((chunks, bj, kt * UNIT), BF16),
            pltpu.VMEM((wn, cl // 2, lanes), F32),
            pltpu.VMEM((wn, cl // 2, lanes), F32),
            pltpu.VMEM((nn, cl // 2, -(-slots * 2 * al // 128) * 128), F32),
            pltpu.VMEM((kt * UNIT, wide_lanes), BF16),
            pltpu.VMEM((kt * UNIT, wide_lanes), BF16),
            pltpu.VMEM((2, wide_lanes // 128, bj, 128), F32),
            pltpu.VMEM((nn, folds, total_tiles) + tile, F32),
            pltpu.VMEM((nn,) + first + tile, F32),
            pltpu.VMEM((nn, pairs - 1, each) + tile, F32),
            pltpu.VMEM((nn, each) + tile, F32),
            pltpu.VMEM((nn, parts, each) + tile, F32),
            pltpu.VMEM((vt, al), F32),
            dma, dma, dma((chunks, wn)), dma((chunks, wn)), dma((chunks,)), dma((chunks,)),
            dma((2, chunks)), dma((nn, chunks)), dma((nn,)), dma((nn,)), dma((nn, pairs - 1)), dma((nn, pairs - 1)),
            dma((nn, parts)), dma((nn, parts)),
        ],
        compiler_params=pltpu.CompilerParams(
            collective_id=ident, has_side_effects=True, vmem_limit_bytes=56 * 1024 * 1024),
    )(amps[0], cycle, irrep_i, irrep_k, irrep_j, irrep_v)
    return result.reshape(1, 1, al, vt)


def general_path(amps, cycle, irrep_i, irrep_k, irrep_j, irrep_v):
    wide_pos = lax.axis_index("wide")
    narrow_pos = lax.axis_index("narrow")
    wide_count = lax.axis_size("wide")
    narrow_count = lax.axis_size("narrow")
    i_total = amps.shape[0]
    k_local = amps.shape[1]
    a_local = amps.shape[2]
    v_total = amps.shape[3]
    k_total = cycle.shape[0]
    c_local = cycle.shape[1]
    b_local = v_total // narrow_count
    j_total = cycle.shape[2] // b_local
    j_local = j_total // wide_count
    cycle_four = cycle.reshape(k_total, c_local, b_local, j_total)
    k_labels = lax.dynamic_slice_in_dim(irrep_k, wide_pos * k_local, k_local)
    a_labels = lax.dynamic_slice_in_dim(irrep_v, narrow_pos * a_local, a_local)
    allowed_in = (
        irrep_i[:, None, None, None]
        ^ k_labels[None, :, None, None]
        ^ a_labels[None, None, :, None]
        ^ irrep_v[None, None, None, :]
        == 0
    )
    masked = jnp.where(allowed_in, amps, jnp.zeros_like(amps))
    moved = lax.all_to_all(masked, "wide", split_axis=3, concat_axis=1, tiled=True)
    piece = lax.all_gather(moved, "narrow", axis=2, tiled=True)
    part_sum = jnp.einsum("ikac,kcbj->iajb", piece, cycle_four, precision=lax.Precision.HIGHEST)
    terms = part_sum.reshape(piece.shape[0], piece.shape[2], j_total * b_local)
    summed = lax.psum_scatter(terms, "wide", scatter_dimension=2, tiled=True)
    summed_four = summed.reshape(i_total, v_total, j_local, b_local)
    j_labels = lax.dynamic_slice_in_dim(irrep_j, wide_pos * j_local, j_local)
    b_labels = lax.dynamic_slice_in_dim(irrep_v, narrow_pos * b_local, b_local)
    allowed_out = (
        irrep_i[:, None, None, None]
        ^ irrep_v[None, :, None, None]
        ^ j_labels[None, None, :, None]
        ^ b_labels[None, None, None, :]
        == 0
    )
    result = jnp.where(allowed_out, summed_four, jnp.zeros_like(summed_four)).reshape(
        i_total, v_total, j_local * b_local
    )
    returned = lax.all_to_all(result, "narrow", split_axis=1, concat_axis=2, tiled=True)
    spread = returned.reshape(i_total, a_local, narrow_count, j_local, b_local)
    return jnp.transpose(spread, (0, 3, 1, 2, 4)).reshape(i_total, j_local, a_local, v_total)


def level_kernel(labels_k, labels_j, out):
    def larger(labels, size):
        over = jnp.int32(0)
        for k in range(size, labels.shape[0]):
            over = over | jnp.where(labels[k] == labels[k - size], 1, 0)
        return over

    level = jnp.int32(0)
    missed = jnp.int32(1)
    for slots, folds in VARIANTS[:-1]:
        missed = missed & (larger(labels_k, slots) | larger(labels_j, folds))
        level = level + missed
    out[0] = level


def per_device(amps, cycle, irrep_i, irrep_k, irrep_j, irrep_v):
    wn = lax.axis_size("wide")
    nn = lax.axis_size("narrow")
    kt, cl, bj = cycle.shape
    al = amps.shape[2]
    bl = amps.shape[3] // nn
    fits = (amps.shape[0] == 1 and wn == 8 and nn == 4 and bj == bl * wn and bl == al and amps.shape[1] == 2
            and kt == 2 * wn and cl == 5 * UNIT and al == 160 and bj % ROWS == 0)
    if not fits:
        return general_path(amps, cycle, irrep_i, irrep_k, irrep_j, irrep_v)
    smem = pl.BlockSpec(memory_space=pltpu.SMEM)
    level = pl.pallas_call(
        level_kernel,
        out_shape=jax.ShapeDtypeStruct((1,), jnp.int32),
        in_specs=[smem, smem],
        out_specs=smem,
    )(irrep_k, irrep_j)[0]
    paths = [functools.partial(packed_path, *sizes, n) for n, sizes in enumerate(VARIANTS)]
    return lax.switch(level, paths, amps, cycle, irrep_i, irrep_k, irrep_j, irrep_v)


def solution(mesh):
    placed = (P(None, "wide", "narrow", None), P(None, "wide", "narrow"), P(), P(), P(), P())
    return jax.shard_map(
        per_device,
        mesh=mesh,
        in_specs=placed,
        out_specs=P(None, "wide", "narrow", None),
        check_vma=False,
    )
```
